32 devices in a mesh: expert: 8 (over z, y), mp: 4 (over x, core).
Axes of the slice: x: 2, y: 2, z: 4, core: 2. Of those that a mesh axis runs over, the one named last changes fastest.
Arguments:
- queries: bfloat16 [256, 48, 128], P('expert', 'mp'), may hold values from -140 to 140
- k_cache: bfloat16 [256, 8, 128, 128], P('expert', 'mp'), may hold values from -5 to 5
- v_cache: bfloat16 [256, 8, 128, 128], P('expert', 'mp'), may hold values from -6 to 6
- lengths: int32 [256], P('expert'), may hold values from 2 to 128
- moe_input: bfloat16 [256, 6144], P('expert', 'mp'), may hold values from -40 to 40
- norm_gain: float32 [6144], P('mp'), may hold values from 0.5 to 1.5
- expert_ids: int32 [256, 2], P('expert'), may hold values from 0 to 7, all different within a row; in each aligned block of 32 rows (0 to 31, 32 to 63, ...) at most 16 rows name the same one
- combine_weights: float32 [256, 2], P('expert'), may hold values from 0.1 to 1
- capacity: int32 [8], replicated, may hold values from 8 to 16
- w_gate: bfloat16 [8, 6144, 8192], P('expert', None, 'mp'), may hold values from -0.078125 to 0.078125
- w_up: bfloat16 [8, 6144, 8192], P('expert', None, 'mp'), may hold values from -0.078125 to 0.078125
- w_down: bfloat16 [8, 8192, 6144], P('expert', 'mp'), may hold values from -0.0625 to 0.0625
Outputs:
- context: bfloat16 [256, 48, 128], P('expert', 'mp')
- layer_out: bfloat16 [256, 6144], P('expert', 'mp')
The draws below stay inside these ranges and needn't reach their ends.
Inputs may be any that keep to these rules, and one draw needn't show every extreme that they name: `expert_ids`: within each aligned block of 32 tokens, no expert is named by more than 16 tokens; the 2 ids of a token differ.
All inputs are finite; a program needn't handle non-finite values.
Results may differ from the reference program's by a relative error of at most 0.007.
Values may be sent and summed in bfloat16 or wider, within the bound.
No kernel may reach another device: no remote copies, remote signals or barrier semaphores. Data moves between devices by JAX's collectives and lax.ppermute only.
A program may use at most 128 MiB of HBM per device.

```python
import math
import jax
import jax.numpy as jnp
import numpy as np
from jax import lax

D = 6144
HEADS = 48
KV_HEADS = 8
HEAD_DIM = 128
FFW = 8192
EXPERTS = 8
TOP = 2
TOK_DEV = 32
LMAX = 128
CAP = 16
SPLIT = 1
TOKENS = 256
BATCH = 256
N_EXPERT = 8


def key_table(key):
    keys = jnp.clip(jax.random.normal(jax.random.fold_in(key, 11), (BATCH, KV_HEADS, LMAX, HEAD_DIM), jnp.float32), -5.0, 5.0)
    return keys


def draw_k_cache(key, part):
    return key_table(key).astype(jnp.bfloat16)


def draw_queries(key, part):
    values = jnp.clip(jax.random.normal(jax.random.fold_in(key, 23), (BATCH, HEADS, HEAD_DIM), jnp.float32), -5.0, 5.0)
    return values.astype(jnp.bfloat16)


def draw_moe_input(key, part):
    base = jnp.clip(jax.random.normal(jax.random.fold_in(key, 5), (TOKENS, D), jnp.float32), -4.0, 4.0)
    rough = jax.random.uniform(jax.random.fold_in(key, 6), (D,), jnp.float32, 0.8, 1.25)
    column = 0.25 * 10.0 ** (jnp.arange(D).astype(jnp.float32) / D) * rough
    values = base * column[None, :]
    return values.astype(jnp.bfloat16)


def plant(array, rng, low, largest):
    longest = array.shape.index(max(array.shape))
    spots = []
    for shift in (0, 1):
        where = [jax.random.randint(jax.random.fold_in(rng, axis), (), 0, length) for axis, length in enumerate(array.shape)]
        where[longest] = (where[longest] + shift) % array.shape[longest]
        spots.append(tuple(where))
    return array.at[spots[0]].set(low).at[spots[1]].set(largest)


def block_levels(own_key, dims, pieces, least, largest):
    level = 1.0
    for dim, parts in pieces:
        draws = jax.random.uniform(jax.random.fold_in(jax.random.fold_in(own_key, 6), dim), (parts,), jnp.float32, least / len(pieces), largest / len(pieces))
        level = level * jnp.repeat(jnp.exp(draws), dims[dim] // parts).reshape((-1,) + (1,) * (len(dims) - 1 - dim))
    return level


def shared_out(rng, own, number, rows, number_of, top, limit, lean):
    ranking = jax.random.permutation(rng, number_of)
    heavy_load, usual = shares(number_of, rows * top, limit, lean, True), shares(number_of, rows * top, limit, lean, False)
    places = jnp.arange(number_of)

    def named(tallies, offset_by):
        used = int((tallies > 0).sum())
        fixed = max(1, used // 4)
        shifted = fixed + (places - fixed + offset_by * (used - fixed)) % max(1, number_of - fixed)
        return jnp.zeros((number_of,), jnp.int32).at[ranking[jnp.where(places < fixed, places, shifted)]].set(jnp.asarray(tallies, jnp.int32))

    tallies = jnp.where(number % 4 == 0, named(heavy_load, number // 4), named(usual, number - number // 4 - 1))
    mixed = jax.random.permutation(jax.random.fold_in(own, 3), number_of)
    giver, receiver = mixed[0:number_of // 2 * 2:2], mixed[1:number_of // 2 * 2:2]
    slack = jnp.minimum(tallies[giver] - 1, limit - tallies[receiver]) // 2
    slack = jnp.where((giver == ranking[0]) | (receiver == ranking[0]) | (tallies[receiver] == 0), 0, jnp.maximum(slack, 0))
    shifted = jax.random.randint(jax.random.fold_in(own, 4), (number_of // 2,), 0, 1 << 20) % (slack + 1)
    tallies = tallies.at[giver].add(-shifted).at[receiver].add(shifted)
    members = jnp.searchsorted(jnp.cumsum(tallies), jnp.arange(rows * top), side="right").astype(jnp.int32)
    grid = members.reshape(top, rows).T
    grid = grid[jax.random.permutation(jax.random.fold_in(own, 1), rows)]
    offset_by = jax.random.randint(jax.random.fold_in(own, 2), (rows, 1), 0, top)
    return jnp.take_along_axis(grid, (jnp.arange(top)[None, :] + offset_by) % top, axis=1)


def shares(amount, total, bound, slope, full):
    loads = [(1 << 20) // math.isqrt(rank ** slope) + 1 for rank in range(1, amount + 1)]
    largest = bound if full else min(bound, max(-(-total // amount), total * loads[0] // sum(loads)))
    least = 1 if total - largest >= amount - 1 else 0
    holding, spare = [largest] + [least] * (amount - 1), total - largest - least * (amount - 1)
    while spare > 0:
        movable = [i for i in range(1, amount) if holding[i] < largest] or [i for i in range(1, amount) if holding[i] < bound]
        mass, left = sum([loads[i] for i in movable]), spare
        for i in movable:
            extra = min(bound - holding[i], max(1, left * loads[i] // mass), spare)
            holding[i] = holding[i] + extra
            spare = spare - extra
    return np.array(holding)


def scatter_about(own_key, extent, deviation, bound, shards=(), dtype=jnp.bfloat16):
    entries = jax.random.normal(own_key, extent, jnp.float32) * deviation
    if len(shards) > 0:
        entries = block_levels(own_key, extent, shards, -0.22, 0.18) * entries
    return jnp.clip(entries, min=-bound, max=bound).astype(dtype)


def setup_inputs(seed: int = 0) -> dict:
    streams_of = jax.random.split(jax.random.key(seed), 13)
    queries = draw_queries(jax.random.fold_in(streams_of[12], 71), 0)
    k_cache = draw_k_cache(jax.random.fold_in(streams_of[12], 71), 0)
    v_cache = scatter_about(streams_of[2], (BATCH, KV_HEADS, LMAX, HEAD_DIM), 1.0, 6.0, ((0, 8), (1, 4)))
    lengths = plant(jax.random.randint(streams_of[3], (BATCH,), 2, LMAX + 1), jax.random.fold_in(streams_of[3], 1), 2, LMAX).astype(jnp.int32)
    moe_input = draw_moe_input(jax.random.fold_in(streams_of[12], 71), 0)
    norm_gain = jnp.clip(1.0 + 0.1 * jax.random.normal(streams_of[5], (D,), jnp.float32), 0.5, 1.5)
    expert_ids_keys = jax.random.split(jax.random.fold_in(streams_of[6], 1), TOKENS // TOK_DEV)
    expert_ids_turns = jax.random.permutation(jax.random.fold_in(streams_of[6], 3), TOKENS // TOK_DEV)
    expert_ids = jax.vmap(lambda own, number: shared_out(jax.random.fold_in(streams_of[6], 2), own, number, TOK_DEV, EXPERTS, TOP, CAP, 2))(expert_ids_keys, expert_ids_turns).reshape((TOKENS, TOP))
    combine_weights = jnp.clip(0.1 + 0.9 * jax.random.uniform(streams_of[7], (TOKENS, TOP), jnp.float32) ** block_levels(streams_of[7], (TOKENS, TOP), ((0, 8),), -0.2, 0.2), 0.1, 1.0)
    capacity = plant(jax.random.randint(streams_of[8], (EXPERTS,), CAP // 2, CAP + 1), jax.random.fold_in(streams_of[8], 1), CAP // 2, CAP).astype(jnp.int32)
    w_gate = scatter_about(streams_of[9], (EXPERTS * SPLIT, D, FFW // SPLIT), D ** -0.5, 0.078125, ((0, 8), (2, 4)))
    w_up = scatter_about(streams_of[10], (EXPERTS * SPLIT, D, FFW // SPLIT), D ** -0.5, 0.078125, ((0, 8), (2, 4)))
    w_down = scatter_about(streams_of[11], (EXPERTS * SPLIT, FFW // SPLIT, D), FFW ** -0.5, 0.0625, ((0, 8), (1, 4)))
    return {"queries": queries, "k_cache": k_cache, "v_cache": v_cache, "lengths": lengths, "moe_input": moe_input, "norm_gain": norm_gain, "expert_ids": expert_ids, "combine_weights": combine_weights, "capacity": capacity, "w_gate": w_gate, "w_up": w_up, "w_down": w_down}


def reference(queries, k_cache, v_cache, lengths, moe_input, norm_gain, expert_ids, combine_weights, capacity, w_gate, w_up, w_down):
    group_size = HEADS // KV_HEADS
    queries_grouped = queries.astype(jnp.float32).reshape(BATCH, KV_HEADS, group_size, HEAD_DIM)
    scores = jnp.einsum('bjgd,bjpd->bjgp', queries_grouped, k_cache.astype(jnp.float32)) * HEAD_DIM ** (-0.5)
    live_mask = jnp.arange(LMAX).astype(jnp.int32)[None, :] < lengths[:, None]
    scores = jnp.where(live_mask[:, None, None, :], scores, -jnp.inf)
    top_score = lax.optimization_barrier(jnp.max(scores, axis=-1, keepdims=True))
    expo = jnp.exp(scores - top_score)
    probs = (expo / lax.optimization_barrier(jnp.sum(expo, axis=-1, keepdims=True))).astype(jnp.bfloat16)
    context = jnp.einsum('bjgp,bjpd->bjgd', probs.astype(jnp.float32), v_cache.astype(jnp.float32))
    context = context.astype(jnp.bfloat16).reshape(BATCH, HEADS, HEAD_DIM)
    residual = moe_input.astype(jnp.float32)
    mean_square = lax.optimization_barrier(jnp.mean(residual * residual, axis=-1))
    normed = (residual * lax.rsqrt(mean_square + 1e-05)[:, None] * norm_gain[None, :]).astype(jnp.bfloat16)
    flat_ids = expert_ids.reshape(-1)
    one_hot = (flat_ids[:, None] == jnp.arange(EXPERTS).astype(jnp.int32)[None, :]).astype(jnp.int32)
    blocked = one_hot.reshape(N_EXPERT, TOK_DEV * TOP, EXPERTS)
    earlier = (jnp.cumsum(blocked, axis=1).astype(jnp.int32) - blocked).reshape(-1, EXPERTS)
    slot_rank = lax.optimization_barrier(jnp.sum(earlier * one_hot, axis=1)).astype(jnp.int32)
    limits = lax.optimization_barrier(jnp.sum(one_hot * capacity[None, :], axis=1)).astype(jnp.int32)
    kept_mask = slot_rank < limits
    token_index = (jnp.arange(TOKENS * TOP) // TOP).astype(jnp.int32)
    source = (token_index // TOK_DEV).astype(jnp.int32)
    slot_id = (source * CAP + slot_rank).astype(jnp.int32)
    dropped_slot = jnp.where(kept_mask, slot_id, N_EXPERT * CAP).astype(jnp.int32)
    table = jnp.zeros((EXPERTS, N_EXPERT * CAP), jnp.int32).at[flat_ids, dropped_slot].set(token_index, mode='drop')
    filled = jnp.zeros((EXPERTS, N_EXPERT * CAP), jnp.int32).at[flat_ids, dropped_slot].set(1, mode='drop')
    piece_width = FFW // SPLIT
    gate_pieces = w_gate.reshape(EXPERTS, SPLIT, D, piece_width)
    up_pieces = w_up.reshape(EXPERTS, SPLIT, D, piece_width)
    down_rows = w_down.reshape(EXPERTS, FFW, D)

    def expert_block(operands):
        row_index, row_filled, gate_w, up_w, down_w = operands
        picked = jnp.where(row_filled[:, None] > 0, normed[row_index], jnp.zeros((), jnp.bfloat16))
        gate_sum = jnp.concatenate([jnp.dot(picked, gate_w[piece], preferred_element_type=jnp.float32) for piece in range(SPLIT)], axis=1)
        up_sum = jnp.concatenate([jnp.dot(picked, up_w[piece], preferred_element_type=jnp.float32) for piece in range(SPLIT)], axis=1)
        hidden = (jax.nn.silu(gate_sum) * up_sum).astype(jnp.bfloat16)
        return jnp.dot(hidden, down_w, preferred_element_type=jnp.float32)
    expert_out = lax.map(expert_block, (table, filled, gate_pieces, up_pieces, down_rows))
    safe_slot = jnp.where(kept_mask, slot_id, 0).astype(jnp.int32)
    chosen_out = expert_out[flat_ids, safe_slot]
    coefficient = combine_weights.reshape(-1) * kept_mask.astype(jnp.float32)
    added = (chosen_out * coefficient[:, None]).reshape(TOKENS, TOP, D).sum(axis=1)
    layer_out = (residual + added).astype(jnp.bfloat16)
    return (context, layer_out)
```

```python
import functools

import jax
import jax.numpy as jnp
from jax import lax
from jax.experimental import pallas as pl
from jax.experimental.pallas import tpu as pltpu
from jax.sharding import PartitionSpec as P

TOP = 2
CHUNK = 256
BUFFERS = 6
VMEM_ROWS = 128
ROUTE_FLOPS = 2e10
PACK_FLOPS = 2e10
EXPERT_MIB = 9


IN_VMEM = pl.BlockSpec(memory_space=pltpu.VMEM)
IN_PLACE = pl.BlockSpec(memory_space=pl.ANY)


def attention(queries, k_cache, v_cache, lengths):
    seq_count, head_count, head_size = queries.shape
    kv_count = k_cache.shape[1]
    group_size = head_count // kv_count
    queries_grouped = queries.reshape(seq_count, kv_count, group_size, head_size)
    scores = jnp.einsum(
        "bjgd,bjpd->bjgp", queries_grouped, k_cache, preferred_element_type=jnp.float32
    ) * head_size ** (-0.5)
    positions = jnp.arange(k_cache.shape[2])
    live_mask = positions[None, :] < lengths[:, None]
    scores = jnp.where(live_mask[:, None, None, :], scores, -jnp.inf)
    top_score = jnp.max(scores, axis=-1, keepdims=True)
    expo = jnp.exp(scores - top_score)
    probs = (expo / jnp.sum(expo, axis=-1, keepdims=True)).astype(jnp.bfloat16)
    context = jnp.einsum("bjgp,bjpd->bjgd", probs, v_cache, preferred_element_type=jnp.float32)
    return context.astype(jnp.bfloat16).reshape(seq_count, head_count, head_size)


def position():
    member = lax.axis_index("mp")
    return member, member % 2, member // 2


def route_kernel(rounds, slots, split, ids_at, weights_at, cap_at, select, weighted, ids, weights, cap, sems):
    loads = [
        pltpu.make_async_copy(ids_at, ids, sems.at[0]),
        pltpu.make_async_copy(weights_at, weights, sems.at[1]),
        pltpu.make_async_copy(cap_at, cap, sems.at[2]),
    ]
    for load in loads:
        load.start()
    core, block = position()[1], lax.axis_index("expert")
    rows, tokens = select.shape
    row = lax.broadcasted_iota(jnp.int32, (rows, tokens), 0)
    step = row // slots
    slot = row - step * slots
    expert = jnp.bitwise_xor(block, 2 * step + core) // split
    before = lax.broadcasted_iota(jnp.int32, (tokens, tokens), 0)
    after = lax.broadcasted_iota(jnp.int32, (tokens, tokens), 1)
    earlier = (before < after).astype(jnp.float32)
    for load in loads:
        load.wait()
    first = ids[0:1, :] == expert
    named = first | (ids[1:2, :] == expert)
    rank = jnp.dot(named.astype(jnp.float32), earlier, preferred_element_type=jnp.float32)
    rank = rank.astype(jnp.int32)
    limit = jnp.zeros((rows, tokens), jnp.int32)
    for e in range(cap.shape[0]):
        limit = jnp.where(expert == e, cap[e], limit)
    chosen = named & (rank == slot) & (rank < limit)
    weighted[...] = jnp.where(
        chosen, jnp.where(first, weights[0:1, :], weights[1:2, :]), 0.0
    )
    select[...] = chosen.astype(jnp.float32).astype(jnp.bfloat16)


def pack_kernel(rounds, slots, select, raw, sibling, *sends):
    core = position()[1]
    feat = raw.shape[1]
    for source, place in ((raw, core), (sibling, 1 - core)):
        moved = jnp.dot(select[...], source[...], preferred_element_type=jnp.float32)
        moved = moved.astype(jnp.bfloat16)
        columns = pl.ds(pl.multiple_of(place * feat, 128), feat)
        for k in range(rounds):
            sends[k][:, columns] = moved[k * slots : (k + 1) * slots, :]


def expert_kernel(rounds, slots, *refs):
    gains, refs = refs[:4], refs[4:]
    near_own, refs = refs[:rounds], refs[rounds:]
    far_own, refs = refs[:rounds], refs[rounds:]
    near_sib, refs = refs[:rounds], refs[rounds:]
    far_sib, refs = refs[:rounds], refs[rounds:]
    w_gate, w_up, w_down, own, sib, gain, rows_in, hidden, held, sems = refs
    half = rounds * slots
    width = near_own[0].shape[1]
    depth = rows_in.shape[1]
    feat = gains[0].shape[1]
    hid = w_gate.shape[1]
    member, _, plane = position()
    steps = depth // CHUNK

    def load(j):
        slot = lax.rem(j, BUFFERS)
        columns = pl.ds(pl.multiple_of(j * CHUNK, CHUNK), CHUNK)
        return pltpu.make_async_copy(w_down.at[:, columns], held.at[slot], sems.at[slot])

    for j in range(min(BUFFERS, steps)):
        load(j).start()

    for i in range(4):
        place = jnp.bitwise_xor(member, i)
        gain[:, pl.ds(pl.multiple_of(place * feat, 128), feat)] = gains[i][...]
    near = plane * width
    far = (1 - plane) * width
    piece = 512
    for base, nears, fars in ((0, near_own, far_own), (half, near_sib, far_sib)):
        for k in range(rounds):
            total = jnp.zeros((slots, 128), jnp.float32)
            for part in (nears[k], fars[k]):
                for j in range(width // 128):
                    v = part[:, j * 128 : (j + 1) * 128].astype(jnp.float32)
                    total = total + v * v
            mean = jnp.sum(total, axis=1, keepdims=True) / depth
            scale = lax.rsqrt(mean + 1e-05)
            at = slice(base + k * slots, base + (k + 1) * slots)
            for part, start in ((nears[k], near), (fars[k], far)):
                for j in range(width // piece):
                    columns = pl.ds(pl.multiple_of(start + j * piece, 128), piece)
                    v = part[:, j * piece : (j + 1) * piece].astype(jnp.float32)
                    rows_in[at, columns] = (v * scale * gain[:, columns]).astype(jnp.bfloat16)

    @pl.loop(0, hid // CHUNK)
    def _(j):
        columns = pl.ds(pl.multiple_of(j * CHUNK, CHUNK), CHUNK)
        gate = jnp.dot(rows_in[...], w_gate[:, columns], preferred_element_type=jnp.float32)
        up = jnp.dot(rows_in[...], w_up[:, columns], preferred_element_type=jnp.float32)
        hidden[:, columns] = (gate / (1.0 + jnp.exp(-gate)) * up).astype(jnp.bfloat16)

    @pl.loop(0, steps)
    def _(j):
        slot = lax.rem(j, BUFFERS)
        load(j).wait()
        out = jnp.dot(hidden[...], held[slot], preferred_element_type=jnp.float32)
        columns = pl.ds(pl.multiple_of(j * CHUNK, CHUNK), CHUNK)
        own[:, columns] = out[:half, :]
        sib[:, columns] = out[half:, :].astype(jnp.bfloat16)

        @pl.when(j + BUFFERS < steps)
        def _():
            load(j + BUFFERS).start()


def merge_kernel(rounds, slots, own, arrived, *outs):
    sends, kept = outs[:rounds], outs[rounds:]
    width = kept[0].shape[1]
    plane = position()[2]
    away = pl.ds(pl.multiple_of((1 - plane) * width, 128), width)
    here = pl.ds(pl.multiple_of(plane * width, 128), width)
    for k in range(rounds):
        at = slice(k * slots, (k + 1) * slots)
        sends[k][...] = (own[at, away] + arrived[at, away].astype(jnp.float32)).astype(
            jnp.bfloat16
        )
        kept[k][...] = own[at, here] + arrived[at, here].astype(jnp.float32)


def fold_kernel(kept, crossed, out):
    out[...] = (kept[...] + crossed[...].astype(jnp.float32)).astype(jnp.bfloat16)


def combine_kernel(rounds, slots, weighted, residual, *refs):
    backs, (mine, send, total) = refs[:rounds], refs[rounds:]
    feat = residual.shape[1]
    core = position()[1]
    rows = jnp.concatenate([b[...].astype(jnp.float32) for b in backs], axis=0)
    total[...] = lax.dot_general(
        weighted[...],
        rows,
        (((0,), (0,)), ((), ())),
        precision=lax.Precision.HIGHEST,
        preferred_element_type=jnp.float32,
    )
    here = pl.ds(pl.multiple_of(core * feat, 128), feat)
    away = pl.ds(pl.multiple_of((1 - core) * feat, 128), feat)
    mine[...] = residual[...].astype(jnp.float32) + total[:, here]
    send[...] = total[:, away]


def held(*shape, dtype=jnp.bfloat16):
    return pltpu.VMEM(shape, dtype)


def in_vmem(v):
    return pltpu.with_memory_space_constraint(v, pltpu.VMEM)


def in_hbm(v):
    return pltpu.with_memory_space_constraint(v, pltpu.HBM)


def call(body, name, args, specs, outs, scratch=(), mib=2, flops=0, moved=0):
    return pl.pallas_call(
        body,
        out_shape=outs,
        in_specs=specs,
        out_specs=[IN_VMEM] * len(outs),
        scratch_shapes=list(scratch),
        compiler_params=pltpu.CompilerParams(vmem_limit_bytes=mib << 20),
        cost_estimate=pl.CostEstimate(
            flops=int(flops), bytes_accessed=int(moved), transcendentals=0
        ),
        name=name,
    )(*args)


def expert_layer(
    context, moe_input, norm_gain, expert_ids, combine_weights, capacity, w_gate, w_up, w_down
):
    devices, members = lax.axis_size("expert"), lax.axis_size("mp")
    tokens, feat = moe_input.shape
    split = devices // capacity.shape[0]
    slots = tokens // 2
    rounds = devices // 2
    rows = rounds * slots
    width, depth = 2 * feat, members * feat
    hid = w_gate.shape[2]
    order = range(rounds)
    f32 = jnp.float32

    def across(v, bit):
        return lax.ppermute(v, "mp", [(i, i ^ bit) for i in range(members)])

    def between(v, k):
        pairs = [
            (e * members + m, (e ^ (2 * k + m % 2)) * members + m)
            for e in range(devices)
            for m in range(members)
        ]
        return lax.ppermute(v, ("expert", "mp"), pairs)

    sibling = across(moe_input, 1)
    gain = norm_gain[None, :]
    gain_sib = across(gain, 1)
    gain_far = across(gain, 2)
    select, weighted = call(
        functools.partial(route_kernel, rounds, slots, split),
        "route",
        [in_hbm(expert_ids.T), in_hbm(combine_weights.T), in_hbm(capacity)],
        [IN_PLACE] * 3,
        [held(rows, tokens), held(rows, tokens, dtype=f32)],
        scratch=[
            pltpu.VMEM((TOP, tokens), jnp.int32),
            pltpu.VMEM((TOP, tokens), f32),
            pltpu.SMEM(capacity.shape, jnp.int32),
            pltpu.SemaphoreType.DMA((3,)),
        ],
        flops=ROUTE_FLOPS,
        moved=1e5,
    )
    sibling, gain_sib, gain_far = lax.optimization_barrier((sibling, gain_sib, gain_far))
    sends = call(
        functools.partial(pack_kernel, rounds, slots),
        "pack",
        [select, moe_input, sibling],
        [IN_VMEM] * 3,
        [held(slots, width)] * rounds,
        flops=PACK_FLOPS,
        moved=1e6,
    )
    near_own = [between(sends[k], k) for k in order]

    gain_both = across(gain_far, 1)
    gains = [gain, gain_sib, gain_far, gain_both]

    far_own = [across(near_own[k], 2) for k in order]
    near_sib = [across(near_own[k], 1) for k in order]
    far_sib = [across(far_own[k], 1) for k in order]

    arrivals = [in_vmem(v) for v in near_own + far_own + near_sib + far_sib]
    own, sib = call(
        functools.partial(expert_kernel, rounds, slots),
        "experts",
        [*gains, *arrivals, in_vmem(w_gate[0]), in_vmem(w_up[0]), in_hbm(w_down[0])],
        [IN_VMEM] * (4 + 4 * rounds + 2) + [IN_PLACE],
        [held(rows, depth, dtype=f32), held(rows, depth)],
        scratch=[
            pltpu.VMEM((1, depth), f32),
            pltpu.VMEM((2 * rows, depth), jnp.bfloat16),
            pltpu.VMEM((2 * rows, hid), jnp.bfloat16),
            pltpu.VMEM((BUFFERS, hid, CHUNK), jnp.bfloat16),
            pltpu.SemaphoreType.DMA((BUFFERS,)),
        ],
        mib=EXPERT_MIB,
        flops=12 * rows * depth * hid,
        moved=2 * depth * hid,
    )

    arrived = across(sib, 1)
    merged = call(
        functools.partial(merge_kernel, rounds, slots),
        "merge",
        [own, arrived],
        [IN_VMEM] * 2,
        [held(slots, width)] * rounds + [held(slots, width, dtype=f32)] * rounds,
        flops=rows * depth,
        moved=10 * rows * depth,
    )
    backs = []
    for k in order:
        (summed,) = call(
            fold_kernel,
            "fold",
            [merged[rounds + k], across(merged[k], 2)],
            [IN_VMEM] * 2,
            [held(slots, width)],
            flops=slots * width,
            moved=8 * slots * width,
        )
        backs.append(between(summed, k))
    backs, context = lax.optimization_barrier((backs, context))
    mine, send = call(
        functools.partial(combine_kernel, rounds, slots),
        "combine",
        [weighted, moe_input, *backs],
        [IN_VMEM] * (2 + rounds),
        [held(tokens, feat, dtype=f32)] * 2,
        scratch=[pltpu.VMEM((tokens, width), f32)],
        mib=4,
        flops=2 * rows * tokens * width,
        moved=4 * rows * width,
    )
    return context, (mine + across(send, 1)).astype(jnp.bfloat16)


def gathered_layer(
    context, moe_input, norm_gain, expert_ids, combine_weights, capacity, w_gate, w_up, w_down
):
    tok_rows, feat_width = moe_input.shape
    experts = capacity.shape[0]
    depth = feat_width * lax.axis_size("mp")
    experts_total = lax.axis_size("expert")
    split_count = experts_total // experts
    slot_count = tok_rows // 2
    residual = moe_input.astype(jnp.float32)
    square_sum = lax.psum(jnp.sum(residual * residual, axis=1), "mp")
    normed = (
        residual * lax.rsqrt(square_sum / depth + 1e-05)[:, None] * norm_gain[None, :]
    ).astype(jnp.bfloat16)
    flat_ids = expert_ids.reshape(-1)
    one_hot = (flat_ids[:, None] == jnp.arange(experts)[None, :]).astype(jnp.int32)
    earlier = jnp.cumsum(one_hot, axis=0) - one_hot
    slot_rank = jnp.sum(earlier * one_hot, axis=1)
    limits = jnp.sum(one_hot * capacity[None, :], axis=1)
    kept_mask = slot_rank < limits
    slot_id = flat_ids * slot_count + slot_rank
    select = (jnp.arange(experts * slot_count)[:, None] == slot_id[None, :]) & kept_mask[None, :]
    chosen = select.reshape(experts * slot_count, tok_rows, TOP).sum(axis=-1).astype(jnp.bfloat16)
    packed = jnp.dot(chosen, normed, preferred_element_type=jnp.float32).astype(jnp.bfloat16)
    packed_view = packed.reshape(experts, 1, slot_count, feat_width)
    outgoing = jnp.broadcast_to(
        packed_view, (experts, split_count, slot_count, feat_width)
    ).reshape(experts_total, slot_count, feat_width)
    arrived = lax.all_to_all(outgoing, "expert", split_axis=0, concat_axis=0, tiled=True)
    slot_rows = arrived.reshape(experts_total * slot_count, feat_width)
    piece = lax.all_gather(slot_rows, "mp", axis=1, tiled=True)
    gate_sum = jnp.dot(piece, w_gate[0], preferred_element_type=jnp.float32)
    up_sum = jnp.dot(piece, w_up[0], preferred_element_type=jnp.float32)
    hidden = (jax.nn.silu(gate_sum) * up_sum).astype(jnp.bfloat16)
    down_terms = jnp.dot(hidden, w_down[0], preferred_element_type=jnp.float32)
    result = lax.psum_scatter(
        down_terms.astype(jnp.bfloat16), "mp", scatter_dimension=1, tiled=True
    )
    result = result.reshape(experts_total, slot_count, feat_width)
    returned = lax.all_to_all(result, "expert", split_axis=0, concat_axis=0, tiled=True)
    gathered = (
        returned.astype(jnp.float32)
        .reshape(experts, split_count, slot_count, feat_width)
        .sum(axis=1)
    )
    weighted = select.astype(jnp.float32) * combine_weights.reshape(-1)[None, :]
    weighted = weighted.reshape(experts * slot_count, tok_rows, TOP).sum(axis=-1)
    added = jnp.dot(
        weighted.T,
        gathered.reshape(experts * slot_count, feat_width),
        precision=lax.Precision.HIGHEST,
        preferred_element_type=jnp.float32,
    )
    return context, (residual + added).astype(jnp.bfloat16)


def on_device(queries, k_cache, v_cache, lengths, moe_input, *rest):
    context = attention(queries, k_cache, v_cache, lengths)
    arriving = lax.axis_size("expert") * (moe_input.shape[0] // 2)
    paired = lax.axis_size("mp") == 4 and lax.axis_size("expert") % 2 == 0
    layer = expert_layer if paired and arriving <= VMEM_ROWS else gathered_layer
    return layer(context, moe_input, *rest)


def solution(mesh):
    in_specs = (
        P("expert", "mp", None),
        P("expert", "mp", None, None),
        P("expert", "mp", None, None),
        P("expert"),
        P("expert", "mp"),
        P("mp"),
        P("expert", None),
        P("expert", None),
        P(),
        P("expert", None, "mp"),
        P("expert", None, "mp"),
        P("expert", "mp", None),
    )
    out_specs = (P("expert", "mp", None), P("expert", "mp"))
    return jax.shard_map(
        on_device, mesh=mesh, in_specs=in_specs, out_specs=out_specs, check_vma=False
    )
```

```python
import functools

import jax
import jax.numpy as jnp
from jax import lax
from jax.experimental import pallas as pl
from jax.experimental.pallas import tpu as pltpu
from jax.sharding import PartitionSpec as P


TOP = 2
WIDE = 512
DEEP = 256
EARLY = 6
LATER = 3
VMEM_ROWS = 128
ROUTE_FLOPS = 2e10
PACK_FLOPS = 2e10


IN_VMEM = pl.BlockSpec(memory_space=pltpu.VMEM)
IN_PLACE = pl.BlockSpec(memory_space=pl.ANY)


def attention(queries, k_cache, v_cache, lengths):
    seq_count, head_count, head_size = queries.shape
    kv_count = k_cache.shape[1]
    group_size = head_count // kv_count
    queries_grouped = queries.reshape(seq_count, kv_count, group_size, head_size)
    scores = jnp.einsum(
        "bjgd,bjpd->bjgp", queries_grouped, k_cache, preferred_element_type=jnp.float32
    ) * head_size ** (-0.5)
    positions = jnp.arange(k_cache.shape[2])
    live_mask = positions[None, :] < lengths[:, None]
    scores = jnp.where(live_mask[:, None, None, :], scores, -jnp.inf)
    top_score = jnp.max(scores, axis=-1, keepdims=True)
    expo = jnp.exp(scores - top_score)
    probs = (expo / jnp.sum(expo, axis=-1, keepdims=True)).astype(jnp.bfloat16)
    context = jnp.einsum("bjgp,bjpd->bjgd", probs, v_cache, preferred_element_type=jnp.float32)
    return context.astype(jnp.bfloat16).reshape(seq_count, head_count, head_size)


def attend_kernel(scale, seqs, lengths_at, q_at, k_at, v_at, out, lengths, q, k, v, wide, score, prob, sems):
    copies = [
        pltpu.make_async_copy(source, target, sems.at[i])
        for i, (source, target) in enumerate(
            ((lengths_at, lengths), (q_at, q), (k_at, k), (v_at, v))
        )
    ]
    for copy in copies:
        copy.start()
    heads, size = q.shape[0] // seqs, q.shape[1]
    kv = k.shape[1]
    tall = wide.shape[0] // seqs
    group = heads // kv
    positions = k.shape[2]
    row = lax.broadcasted_iota(jnp.int32, (tall, positions), 0)
    lane = lax.broadcasted_iota(jnp.int32, (tall, positions), 1)
    copies[0].wait()
    copies[1].wait()
    wide[: heads * seqs, :] = q[...].astype(jnp.float32)
    wide[heads * seqs :, :] = jnp.zeros(((tall - heads) * seqs, size), jnp.float32)
    copies[2].wait()
    for b in range(seqs):
        queries = wide[pl.ds(b, tall, stride=seqs), :].astype(jnp.bfloat16)
        total = None
        for j in range(kv):
            dots = lax.dot_general(
                queries,
                k[b, j],
                (((1,), (1,)), ((), ())),
                preferred_element_type=jnp.float32,
            )
            total = dots if total is None else jnp.where(row < j * group, total, dots)
        live = lane < lengths[b]
        score[b * tall : (b + 1) * tall, :] = jnp.where(live, total * scale, -jnp.inf)
    top = jnp.max(score[...], axis=-1, keepdims=True)
    expo = jnp.exp(score[...] - top)
    prob[...] = (expo / jnp.sum(expo, axis=-1, keepdims=True)).astype(jnp.bfloat16)
    copies[3].wait()
    for b in range(seqs):
        probs = prob[b * tall : (b + 1) * tall, :].astype(jnp.float32)
        total = jnp.zeros((tall, size), jnp.float32)
        for j in range(kv):
            mine = (row >= j * group) & (row < (j + 1) * group)
            total = total + jnp.dot(
                jnp.where(mine, probs, 0.0).astype(jnp.bfloat16),
                v[b, j],
                preferred_element_type=jnp.float32,
            )
        wide[pl.ds(b, tall, stride=seqs), :] = total
    out[...] = wide[: heads * seqs, :].astype(jnp.bfloat16)


def position():
    member = lax.axis_index("mp")
    return member, member % 2, member // 2


def route_kernel(slots, split, ids_at, weights_at, cap_at, select, weighted, ids, weights, cap, sems):
    loads = [
        pltpu.make_async_copy(ids_at, ids, sems.at[0]),
        pltpu.make_async_copy(weights_at, weights, sems.at[1]),
        pltpu.make_async_copy(cap_at, cap, sems.at[2]),
    ]
    for load in loads:
        load.start()
    core, block = position()[1], lax.axis_index("expert")
    rows, tokens = select.shape
    row = lax.broadcasted_iota(jnp.int32, (rows, tokens), 0)
    step = row // slots
    slot = row - step * slots
    expert = jnp.bitwise_xor(block, 2 * step + core) // split
    before = lax.broadcasted_iota(jnp.int32, (tokens, tokens), 0)
    after = lax.broadcasted_iota(jnp.int32, (tokens, tokens), 1)
    earlier = (before < after).astype(jnp.float32)
    for load in loads:
        load.wait()
    first = ids[0:1, :] == expert
    named = first | (ids[1:2, :] == expert)
    rank = jnp.dot(named.astype(jnp.float32), earlier, preferred_element_type=jnp.float32)
    rank = rank.astype(jnp.int32)
    limit = jnp.zeros((rows, tokens), jnp.int32)
    for e in range(cap.shape[0]):
        limit = jnp.where(expert == e, cap[e], limit)
    chosen = named & (rank == slot) & (rank < limit)
    weighted[...] = jnp.where(
        chosen, jnp.where(first, weights[0:1, :], weights[1:2, :]), 0.0
    )
    select[...] = chosen.astype(jnp.float32).astype(jnp.bfloat16)


def pack_kernel(slots, first, width, select, *refs):
    sources, sends = refs[: width // refs[0].shape[1]], refs[width // refs[0].shape[1] :]
    member = position()[0]
    feat = sources[0].shape[1]
    rows = select[first * slots : (first + len(sends)) * slots, :]
    for i, source in enumerate(sources):
        moved = jnp.dot(rows, source[...], preferred_element_type=jnp.float32)
        moved = moved.astype(jnp.bfloat16)
        place = lax.rem(jnp.bitwise_xor(member, i) * feat, width)
        columns = pl.ds(pl.multiple_of(place, 128), feat)
        for k, send in enumerate(sends):
            send[:, columns] = moved[k * slots : (k + 1) * slots, :]


def gain_kernel(own, sibling, across, both, out):
    member = position()[0]
    feat = own.shape[1]
    for i, part in enumerate((own, sibling, across, both)):
        place = jnp.bitwise_xor(member, i)
        out[:, pl.ds(pl.multiple_of(place * feat, 128), feat)] = part[...]


def norm_kernel(*refs):
    parts, (gain, out) = refs[:-2], refs[-2:]
    plane = position()[2]
    width, depth = parts[0].shape[1], out.shape[1]
    starts = (plane * width, (1 - plane) * width) if len(parts) == 2 else (0,)
    total = jnp.zeros((out.shape[0], 128), jnp.float32)
    for part in parts:
        for j in range(width // 128):
            v = part[:, j * 128 : (j + 1) * 128].astype(jnp.float32)
            total = total + v * v
    mean = jnp.sum(total, axis=1, keepdims=True) / depth
    scale = lax.rsqrt(mean + 1e-05)
    for part, start in zip(parts, starts):
        for j in range(0, width, WIDE):
            columns = pl.ds(pl.multiple_of(start + j, 128), WIDE)
            v = part[:, j : j + WIDE].astype(jnp.float32)
            out[:, columns] = (v * scale * gain[:, columns]).astype(jnp.bfloat16)


def half_load(w_down, target, sems, first):
    width = w_down.shape[1] // 2
    blocks = w_down.shape[0] // DEEP
    plane = position()[2]

    def load(i):
        half, block = divmod(first + i, blocks)
        start = (plane if half else 1 - plane) * width
        return pltpu.make_async_copy(
            w_down.at[block * DEEP : (block + 1) * DEEP, pl.ds(pl.multiple_of(start, 128), width)],
            target.at[i * DEEP : (i + 1) * DEEP, :],
            sems.at[i],
        )

    return load


def hidden_kernel(count, *refs):
    rows_in, (w_gate, w_up, w_down, hidden, ahead, sems) = refs[:count], refs[count:]
    load = half_load(w_down, ahead, sems, 0)
    blocks = sems.shape[0]
    for i in range(blocks):
        load(i).start()

    @pl.loop(0, w_gate.shape[1] // WIDE)
    def _(j):
        columns = pl.ds(pl.multiple_of(j * WIDE, WIDE), WIDE)
        rows = jnp.concatenate([r[...] for r in rows_in], axis=0)
        gate = jnp.dot(rows, w_gate[:, columns], preferred_element_type=jnp.float32)
        up = jnp.dot(rows, w_up[:, columns], preferred_element_type=jnp.float32)
        hidden[:, columns] = (gate / (1.0 + jnp.exp(-gate)) * up).astype(jnp.bfloat16)

    for i in range(blocks):
        load(i).wait()


def down_kernel(first, later, hidden, ready, w_down, own, sib, *refs):
    if later:
        ahead, here, total, sems, sems_later = refs
    else:
        here, total, sems = refs
    half, width = own.shape
    known, missing = ready.shape[0], sems.shape[0]
    load = half_load(w_down, here, sems, first + known // DEEP)
    for i in range(missing):
        load(i).start()
    if later:
        load_later = half_load(w_down, ahead, sems_later, first + known // DEEP + missing)
        for i in range(later):
            load_later(i).start()
    for step in range(missing + 1):
        if step == 0:
            left, weight = hidden.at[:, :known], ready
        else:
            load(step - 1).wait()
            at = known + (step - 1) * DEEP
            left = hidden.at[:, at : at + DEEP]
            weight = here.at[(step - 1) * DEEP : step * DEEP, :]
        for j in range(width // WIDE):
            columns = slice(j * WIDE, (j + 1) * WIDE)
            out = jnp.dot(left[...], weight[:, columns], preferred_element_type=jnp.float32)
            if step > 0:
                out = out + total[:, columns]
            if step < missing:
                total[:, columns] = out
            else:
                own[:, columns] = out[:half, :]
                sib[:, columns] = out[half:, :].astype(jnp.bfloat16)
    if later:
        for i in range(later):
            load_later(i).wait()


def merge_kernel(own, arrived, *sends):
    slots = sends[0].shape[0]
    for k, send in enumerate(sends):
        at = slice(k * slots, (k + 1) * slots)
        send[...] = (own[at, :] + arrived[at, :].astype(jnp.float32)).astype(jnp.bfloat16)


def fold_kernel(k, own, arrived, crossed, out):
    slots = out.shape[0]
    at = slice(k * slots, (k + 1) * slots)
    total = own[at, :] + arrived[at, :].astype(jnp.float32)
    out[...] = (total + crossed[...].astype(jnp.float32)).astype(jnp.bfloat16)


def combine_kernel(rounds, weighted, residual, *refs):
    backs, (mine, send, total) = refs[:rounds], refs[rounds:]
    feat = residual.shape[1]
    core = position()[1]
    rows = jnp.concatenate([b[...].astype(jnp.float32) for b in backs], axis=0)
    total[...] = lax.dot_general(
        weighted[...],
        rows,
        (((0,), (0,)), ((), ())),
        precision=lax.Precision.HIGHEST,
        preferred_element_type=jnp.float32,
    )
    here = pl.ds(pl.multiple_of(core * feat, 128), feat)
    away = pl.ds(pl.multiple_of((1 - core) * feat, 128), feat)
    mine[...] = residual[...].astype(jnp.float32) + total[:, here]
    send[...] = total[:, away]


def held(*shape, dtype=jnp.bfloat16):
    return pltpu.VMEM(shape, dtype)


def in_vmem(v):
    return pltpu.with_memory_space_constraint(v, pltpu.VMEM)


def in_hbm(v):
    return pltpu.with_memory_space_constraint(v, pltpu.HBM)


def call(body, args, specs, outs, scratch=(), mib=2, flops=0, moved=0, alias=None):
    return pl.pallas_call(
        body,
        out_shape=outs,
        in_specs=specs,
        out_specs=[IN_VMEM] * len(outs),
        scratch_shapes=list(scratch),
        compiler_params=pltpu.CompilerParams(vmem_limit_bytes=mib << 20),
        cost_estimate=pl.CostEstimate(
            flops=int(flops), bytes_accessed=int(moved), transcendentals=0
        ),
        input_output_aliases=alias or {},
    )(*args)


def expert_layer(
    moe_input, norm_gain, expert_ids, combine_weights, capacity, w_gate, w_up, w_down
):
    devices, members = lax.axis_size("expert"), lax.axis_size("mp")
    tokens, feat = moe_input.shape
    split = devices // capacity.shape[0]
    slots = tokens // 2
    rounds = devices // 2
    rows = rounds * slots
    width, depth = 2 * feat, members * feat
    hid = w_gate.shape[2]
    order = range(rounds)
    f32 = jnp.float32

    def across(v, bit):
        return lax.ppermute(v, "mp", [(i, i ^ bit) for i in range(members)])

    def between(v, k):
        pairs = [
            (e * members + m, (e ^ (2 * k + m % 2)) * members + m)
            for e in range(devices)
            for m in range(members)
        ]
        return lax.ppermute(v, ("expert", "mp"), pairs)

    low = rounds // 2
    sibling = across(moe_input, 1)
    opposite = across(moe_input, 2)
    select, weighted = call(
        functools.partial(route_kernel, slots, split),
        [in_hbm(expert_ids.T), in_hbm(combine_weights.T), in_hbm(capacity)],
        [IN_PLACE] * 3,
        [held(rows, tokens), held(rows, tokens, dtype=f32)],
        scratch=[
            pltpu.VMEM((TOP, tokens), jnp.int32),
            pltpu.VMEM((TOP, tokens), f32),
            pltpu.SMEM(capacity.shape, jnp.int32),
            pltpu.SemaphoreType.DMA((3,)),
        ],
        flops=ROUTE_FLOPS,
        moved=1e5,
    )
    gain, sibling, select = lax.optimization_barrier((norm_gain[None, :], sibling, select))

    def pack(first, count, total, sources):
        return call(
            functools.partial(pack_kernel, slots, first, total),
            [select, *sources],
            [IN_VMEM] * (1 + len(sources)),
            [held(slots, total)] * count,
            flops=PACK_FLOPS,
            moved=1e6,
        )

    high_sends = pack(low, rounds - low, width, [moe_input, sibling])
    near = [between(high_sends[k - low], k) for k in range(low, rounds)]
    diagonal = across(opposite, 1)
    low_sends = pack(0, low, depth, [moe_input, sibling, opposite, diagonal])
    full = [between(low_sends[k], k) for k in range(low)]

    gain, _ = lax.optimization_barrier((gain, high_sends[0]))
    gain_sib = across(gain, 1)
    gain_far = across(gain, 2)
    gain_both = across(gain_far, 1)
    (gains,) = call(
        gain_kernel,
        [gain, gain_sib, gain_far, gain_both],
        [IN_VMEM] * 4,
        [held(1, depth, dtype=f32)],
    )

    normed = []
    for k in order:
        parts = [full[k]] if k < low else [near[k - low], across(near[k - low], 2)]
        normed += call(
            norm_kernel,
            [*parts, gains],
            [IN_VMEM] * (len(parts) + 1),
            [held(slots, depth)],
            flops=8 * slots * depth,
            moved=4 * slots * depth,
        )
    entering = [in_vmem(v) for v in normed + [across(v, 1) for v in normed]]
    blocks = hid // DEEP
    early, later = min(EARLY, blocks - 1), min(LATER, blocks - 1)
    weight = in_hbm(w_down[0])
    hidden, ahead = call(
        functools.partial(hidden_kernel, len(entering)),
        [*entering, in_vmem(w_gate[0]), in_vmem(w_up[0]), weight],
        [IN_VMEM] * (len(entering) + 2) + [IN_PLACE],
        [held(2 * rows, hid), held(early * DEEP, width)],
        scratch=[pltpu.SemaphoreType.DMA((early,))],
        flops=8 * rows * depth * hid,
        moved=2 * early * DEEP * width,
    )

    def down(first, ready, later):
        missing = blocks - ready.shape[0] // DEEP
        ahead = [held(later * DEEP, width)] if later else []
        sems = [pltpu.SemaphoreType.DMA((later,))] if later else []
        return call(
            functools.partial(down_kernel, first, later),
            [in_vmem(hidden), in_vmem(ready), weight],
            [IN_VMEM] * 2 + [IN_PLACE],
            [held(rows, width, dtype=f32), held(rows, width)] + ahead,
            scratch=[
                pltpu.VMEM((missing * DEEP, width), jnp.bfloat16),
                pltpu.VMEM((2 * rows, width), f32),
                pltpu.SemaphoreType.DMA((missing,)),
            ]
            + sems,
            mib=3 + missing * DEEP * width * 2 // 2**20 + 1,
            flops=2 * rows * depth * hid,
            moved=2 * (missing + later) * DEEP * width,
        )

    own_far, sib_far, kept = down(0, ahead, later)
    arrived_far = across(sib_far, 1)
    own_near, sib_near = down(blocks, kept, 0)
    arrived_near = across(sib_near, 1)
    crossing = call(
        merge_kernel,
        [own_far, arrived_far],
        [IN_VMEM] * 2,
        [held(slots, width)] * rounds,
        flops=rows * width,
        moved=8 * rows * width,
    )
    backs = []
    for k in reversed(order):
        (summed,) = call(
            functools.partial(fold_kernel, k),
            [own_near, arrived_near, across(crossing[k], 2)],
            [IN_VMEM] * 3,
            [held(slots, width)],
            flops=slots * width,
            moved=8 * slots * width,
        )
        backs.insert(0, between(summed, k))
    mine, send = call(
        functools.partial(combine_kernel, rounds),
        [weighted, moe_input, *backs],
        [IN_VMEM] * (2 + rounds),
        [held(tokens, feat, dtype=f32)] * 2,
        scratch=[pltpu.VMEM((tokens, width), f32)],
        mib=4,
        flops=2 * rows * tokens * width,
        moved=4 * rows * width,
    )
    return (mine + across(send, 1)).astype(jnp.bfloat16)


def gathered_layer(
    moe_input, norm_gain, expert_ids, combine_weights, capacity, w_gate, w_up, w_down
):
    tok_rows, feat_width = moe_input.shape
    experts = capacity.shape[0]
    depth = feat_width * lax.axis_size("mp")
    experts_total = lax.axis_size("expert")
    split_count = experts_total // experts
    slot_count = tok_rows // 2
    residual = moe_input.astype(jnp.float32)
    square_sum = lax.psum(jnp.sum(residual * residual, axis=1), "mp")
    normed = (
        residual * lax.rsqrt(square_sum / depth + 1e-05)[:, None] * norm_gain[None, :]
    ).astype(jnp.bfloat16)
    flat_ids = expert_ids.reshape(-1)
    one_hot = (flat_ids[:, None] == jnp.arange(experts)[None, :]).astype(jnp.int32)
    earlier = jnp.cumsum(one_hot, axis=0) - one_hot
    slot_rank = jnp.sum(earlier * one_hot, axis=1)
    limits = jnp.sum(one_hot * capacity[None, :], axis=1)
    kept_mask = slot_rank < limits
    slot_id = flat_ids * slot_count + slot_rank
    select = (jnp.arange(experts * slot_count)[:, None] == slot_id[None, :]) & kept_mask[None, :]
    chosen = select.reshape(experts * slot_count, tok_rows, TOP).sum(axis=-1).astype(jnp.bfloat16)
    packed = jnp.dot(chosen, normed, preferred_element_type=jnp.float32).astype(jnp.bfloat16)
    packed_view = packed.reshape(experts, 1, slot_count, feat_width)
    outgoing = jnp.broadcast_to(
        packed_view, (experts, split_count, slot_count, feat_width)
    ).reshape(experts_total, slot_count, feat_width)
    arrived = lax.all_to_all(outgoing, "expert", split_axis=0, concat_axis=0, tiled=True)
    slot_rows = arrived.reshape(experts_total * slot_count, feat_width)
    piece = lax.all_gather(slot_rows, "mp", axis=1, tiled=True)
    gate_sum = jnp.dot(piece, w_gate[0], preferred_element_type=jnp.float32)
    up_sum = jnp.dot(piece, w_up[0], preferred_element_type=jnp.float32)
    hidden = (jax.nn.silu(gate_sum) * up_sum).astype(jnp.bfloat16)
    down_terms = jnp.dot(hidden, w_down[0], preferred_element_type=jnp.float32)
    result = lax.psum_scatter(
        down_terms.astype(jnp.bfloat16), "mp", scatter_dimension=1, tiled=True
    )
    result = result.reshape(experts_total, slot_count, feat_width)
    returned = lax.all_to_all(result, "expert", split_axis=0, concat_axis=0, tiled=True)
    gathered = (
        returned.astype(jnp.float32)
        .reshape(experts, split_count, slot_count, feat_width)
        .sum(axis=1)
    )
    weighted = select.astype(jnp.float32) * combine_weights.reshape(-1)[None, :]
    weighted = weighted.reshape(experts * slot_count, tok_rows, TOP).sum(axis=-1)
    added = jnp.dot(
        weighted.T,
        gathered.reshape(experts * slot_count, feat_width),
        precision=lax.Precision.HIGHEST,
        preferred_element_type=jnp.float32,
    )
    return (residual + added).astype(jnp.bfloat16)


def attend_held(queries, k_cache, v_cache, lengths):
    seqs, heads, size = queries.shape
    tall = -(-heads // 16) * 16
    flat = queries.transpose(1, 0, 2).reshape(heads * seqs, size)
    positions = k_cache.shape[2]
    (out,) = call(
        functools.partial(attend_kernel, size ** (-0.5), seqs),
        [in_hbm(v) for v in (lengths, flat, k_cache, v_cache)],
        [IN_PLACE] * 4,
        [held(heads * seqs, size)],
        scratch=[
            pltpu.SMEM(lengths.shape, jnp.int32),
            pltpu.VMEM(flat.shape, flat.dtype),
            pltpu.VMEM(k_cache.shape, k_cache.dtype),
            pltpu.VMEM(v_cache.shape, v_cache.dtype),
            pltpu.VMEM((tall * seqs, size), jnp.float32),
            pltpu.VMEM((tall * seqs, positions), jnp.float32),
            pltpu.VMEM((tall * seqs, positions), jnp.bfloat16),
            pltpu.SemaphoreType.DMA((4,)),
        ],
        mib=7,
        flops=8 * seqs * tall * size * positions,
        moved=2 * k_cache.size * 2,
    )
    return out.reshape(heads, seqs, size).transpose(1, 0, 2)


def on_device(queries, k_cache, v_cache, lengths, moe_input, *rest):
    arriving = lax.axis_size("expert") * (moe_input.shape[0] // 2)
    paired = lax.axis_size("mp") == 4 and lax.axis_size("expert") % 4 == 0
    if paired and arriving <= VMEM_ROWS:
        context = attend_held(queries, k_cache, v_cache, lengths)
        return context, expert_layer(moe_input, *rest)
    context = attention(queries, k_cache, v_cache, lengths)
    return context, gathered_layer(moe_input, *rest)


def solution(mesh):
    in_specs = (
        P("expert", "mp", None),
        P("expert", "mp", None, None),
        P("expert", "mp", None, None),
        P("expert"),
        P("expert", "mp"),
        P("mp"),
        P("expert", None),
        P("expert", None),
        P(),
        P("expert", None, "mp"),
        P("expert", None, "mp"),
        P("expert", "mp", None),
    )
    out_specs = (P("expert", "mp", None), P("expert", "mp"))
    return jax.shard_map(
        on_device, mesh=mesh, in_specs=in_specs, out_specs=out_specs, check_vma=False
    )
```

```python
import functools

import jax
import jax.numpy as jnp
from jax import lax
from jax.experimental import pallas as pl
from jax.experimental.pallas import tpu as pltpu
from jax.sharding import PartitionSpec as P


TOP = 2
WIDE = 512
DEEP = 256
RING = 8
SPAN = 8
EARLY = 7
LATER = 3
VMEM_ROWS = 128
ROUTE_FLOPS = 2e10
PACK_FLOPS = 2e10


IN_VMEM = pl.BlockSpec(memory_space=pltpu.VMEM)
IN_PLACE = pl.BlockSpec(memory_space=pl.ANY)


def attention(queries, k_cache, v_cache, lengths):
    seq_count, head_count, head_size = queries.shape
    kv_count = k_cache.shape[1]
    group_size = head_count // kv_count
    queries_grouped = queries.reshape(seq_count, kv_count, group_size, head_size)
    scores = jnp.einsum(
        "bjgd,bjpd->bjgp", queries_grouped, k_cache, preferred_element_type=jnp.float32
    ) * head_size ** (-0.5)
    positions = jnp.arange(k_cache.shape[2])
    live_mask = positions[None, :] < lengths[:, None]
    scores = jnp.where(live_mask[:, None, None, :], scores, -jnp.inf)
    top_score = jnp.max(scores, axis=-1, keepdims=True)
    expo = jnp.exp(scores - top_score)
    probs = (expo / jnp.sum(expo, axis=-1, keepdims=True)).astype(jnp.bfloat16)
    context = jnp.einsum("bjgp,bjpd->bjgd", probs, v_cache, preferred_element_type=jnp.float32)
    return context.astype(jnp.bfloat16).reshape(seq_count, head_count, head_size)


def attend_kernel(scale, seqs, lengths_at, q_at, k_at, v_at, out, lengths, q, ring, wide, score, prob, sems):
    span = ring.shape[1]
    parts = seqs // span
    slots = ring.shape[0]
    near = [
        pltpu.make_async_copy(source, target, sems.at[i])
        for i, (source, target) in enumerate(((lengths_at, lengths), (q_at, q)))
    ]

    def load(i):
        source = (k_at if i < parts else v_at).at[i % parts * span : (i % parts + 1) * span]
        return pltpu.make_async_copy(source, ring.at[i % slots], sems.at[2 + i])

    def turn(i):
        if i + slots < 2 * parts:
            load(i + slots).start()

    for copy in near:
        copy.start()
    for i in range(slots):
        load(i).start()
    heads, size = q.shape[0] // seqs, q.shape[1]
    kv = ring.shape[2]
    tall = wide.shape[0] // seqs
    group = heads // kv
    positions = ring.shape[3]
    row = lax.broadcasted_iota(jnp.int32, (tall, positions), 0)
    lane = lax.broadcasted_iota(jnp.int32, (tall, positions), 1)
    for copy in near:
        copy.wait()
    wide[: heads * seqs, :] = q[...].astype(jnp.float32)
    wide[heads * seqs :, :] = jnp.zeros(((tall - heads) * seqs, size), jnp.float32)
    for i in range(parts):
        load(i).wait()
        for at in range(span):
            b = i * span + at
            queries = wide[pl.ds(b, tall, stride=seqs), :].astype(jnp.bfloat16)
            total = None
            for j in range(kv):
                dots = lax.dot_general(
                    queries,
                    ring[i % slots, at, j],
                    (((1,), (1,)), ((), ())),
                    preferred_element_type=jnp.float32,
                )
                total = dots if total is None else jnp.where(row < j * group, total, dots)
            live = lane < lengths[b]
            score[b * tall : (b + 1) * tall, :] = jnp.where(live, total * scale, -jnp.inf)
        turn(i)
    top = jnp.max(score[...], axis=-1, keepdims=True)
    expo = jnp.exp(score[...] - top)
    prob[...] = (expo / jnp.sum(expo, axis=-1, keepdims=True)).astype(jnp.bfloat16)
    for i in range(parts, 2 * parts):
        load(i).wait()
        for at in range(span):
            b = (i - parts) * span + at
            probs = prob[b * tall : (b + 1) * tall, :].astype(jnp.float32)
            total = jnp.zeros((tall, size), jnp.float32)
            for j in range(kv):
                mine = (row >= j * group) & (row < (j + 1) * group)
                total = total + jnp.dot(
                    jnp.where(mine, probs, 0.0).astype(jnp.bfloat16),
                    ring[i % slots, at, j],
                    preferred_element_type=jnp.float32,
                )
            wide[pl.ds(b, tall, stride=seqs), :] = total
        turn(i)
    out[...] = wide[: heads * seqs, :].astype(jnp.bfloat16)


def position():
    member = lax.axis_index("mp")
    return member, member % 2, member // 2


def route_kernel(slots, split, ids_at, weights_at, cap_at, select, weighted, ids, weights, cap, sems):
    loads = [
        pltpu.make_async_copy(ids_at, ids, sems.at[0]),
        pltpu.make_async_copy(weights_at, weights, sems.at[1]),
        pltpu.make_async_copy(cap_at, cap, sems.at[2]),
    ]
    for load in loads:
        load.start()
    core, block = position()[1], lax.axis_index("expert")
    rows, tokens = select.shape
    row = lax.broadcasted_iota(jnp.int32, (rows, tokens), 0)
    step = row // slots
    slot = row - step * slots
    expert = jnp.bitwise_xor(block, 2 * step + core) // split
    before = lax.broadcasted_iota(jnp.int32, (tokens, tokens), 0)
    after = lax.broadcasted_iota(jnp.int32, (tokens, tokens), 1)
    earlier = (before < after).astype(jnp.float32)
    for load in loads:
        load.wait()
    first = ids[0:1, :] == expert
    named = first | (ids[1:2, :] == expert)
    rank = jnp.dot(named.astype(jnp.float32), earlier, preferred_element_type=jnp.float32)
    rank = rank.astype(jnp.int32)
    limit = jnp.zeros((rows, tokens), jnp.int32)
    for e in range(cap.shape[0]):
        limit = jnp.where(expert == e, cap[e], limit)
    chosen = named & (rank == slot) & (rank < limit)
    weighted[...] = jnp.where(
        chosen, jnp.where(first, weights[0:1, :], weights[1:2, :]), 0.0
    )
    select[...] = chosen.astype(jnp.float32).astype(jnp.bfloat16)


def pack_kernel(slots, first, width, select, *refs):
    sources, sends = refs[: width // refs[0].shape[1]], refs[width // refs[0].shape[1] :]
    member = position()[0]
    feat = sources[0].shape[1]
    rows = select[first * slots : (first + len(sends)) * slots, :]
    for i, source in enumerate(sources):
        moved = jnp.dot(rows, source[...], preferred_element_type=jnp.float32)
        moved = moved.astype(jnp.bfloat16)
        place = lax.rem(jnp.bitwise_xor(member, i) * feat, width)
        columns = pl.ds(pl.multiple_of(place, 128), feat)
        for k, send in enumerate(sends):
            send[:, columns] = moved[k * slots : (k + 1) * slots, :]


def gain_kernel(own, sibling, across, both, out):
    member = position()[0]
    feat = own.shape[1]
    for i, part in enumerate((own, sibling, across, both)):
        place = jnp.bitwise_xor(member, i)
        out[:, pl.ds(pl.multiple_of(place * feat, 128), feat)] = part[...]


def norm_kernel(*refs):
    parts, (gain, out) = refs[:-2], refs[-2:]
    plane = position()[2]
    width, depth = parts[0].shape[1], out.shape[1]
    starts = (plane * width, (1 - plane) * width) if len(parts) == 2 else (0,)
    total = jnp.zeros((out.shape[0], 128), jnp.float32)
    for part in parts:
        for j in range(width // 128):
            v = part[:, j * 128 : (j + 1) * 128].astype(jnp.float32)
            total = total + v * v
    mean = jnp.sum(total, axis=1, keepdims=True) / depth
    scale = lax.rsqrt(mean + 1e-05)
    for part, start in zip(parts, starts):
        for j in range(0, width, WIDE):
            columns = pl.ds(pl.multiple_of(start + j, 128), WIDE)
            v = part[:, j : j + WIDE].astype(jnp.float32)
            out[:, columns] = (v * scale * gain[:, columns]).astype(jnp.bfloat16)


def half_load(w_down, target, sems, first):
    width = w_down.shape[1] // 2
    blocks = w_down.shape[0] // DEEP
    plane = position()[2]

    def load(i):
        half, block = divmod(first + i, blocks)
        start = (plane if half else 1 - plane) * width
        return pltpu.make_async_copy(
            w_down.at[block * DEEP : (block + 1) * DEEP, pl.ds(pl.multiple_of(start, 128), width)],
            target.at[i * DEEP : (i + 1) * DEEP, :],
            sems.at[i],
        )

    return load


def hidden_kernel(count, *refs):
    rows_in, (w_gate, w_up, w_down, hidden, ahead, sems) = refs[:count], refs[count:]
    load = half_load(w_down, ahead, sems, 0)
    blocks = sems.shape[0]
    for i in range(blocks):
        load(i).start()

    @pl.loop(0, w_gate.shape[1] // WIDE)
    def _(j):
        columns = pl.ds(pl.multiple_of(j * WIDE, WIDE), WIDE)
        rows = jnp.concatenate([r[...] for r in rows_in], axis=0)
        gate = jnp.dot(rows, w_gate[:, columns], preferred_element_type=jnp.float32)
        up = jnp.dot(rows, w_up[:, columns], preferred_element_type=jnp.float32)
        hidden[:, columns] = (gate / (1.0 + jnp.exp(-gate)) * up).astype(jnp.bfloat16)

    for i in range(blocks):
        load(i).wait()


def down_kernel(first, later, hidden, ready, w_down, own, sib, *refs):
    if later:
        ahead, here, total, sems, sems_later = refs
    else:
        here, total, sems = refs
    half, width = own.shape
    known, missing = ready.shape[0], sems.shape[0]
    load = half_load(w_down, here, sems, first + known // DEEP)
    for i in range(missing):
        load(i).start()
    if later:
        load_later = half_load(w_down, ahead, sems_later, first + known // DEEP + missing)
        for i in range(later):
            load_later(i).start()
    for step in range(missing + 1):
        if step == 0:
            left, weight = hidden.at[:, :known], ready
        else:
            load(step - 1).wait()
            at = known + (step - 1) * DEEP
            left = hidden.at[:, at : at + DEEP]
            weight = here.at[(step - 1) * DEEP : step * DEEP, :]
        for j in range(width // WIDE):
            columns = slice(j * WIDE, (j + 1) * WIDE)
            out = jnp.dot(left[...], weight[:, columns], preferred_element_type=jnp.float32)
            if step > 0:
                out = out + total[:, columns]
            if step < missing:
                total[:, columns] = out
            else:
                own[:, columns] = out[:half, :]
                sib[:, columns] = out[half:, :].astype(jnp.bfloat16)
    if later:
        for i in range(later):
            load_later(i).wait()


def merge_kernel(own, arrived, *sends):
    slots = sends[0].shape[0]
    for k, send in enumerate(sends):
        at = slice(k * slots, (k + 1) * slots)
        send[...] = (own[at, :] + arrived[at, :].astype(jnp.float32)).astype(jnp.bfloat16)


def fold_kernel(k, own, arrived, crossed, out):
    slots = out.shape[0]
    at = slice(k * slots, (k + 1) * slots)
    total = own[at, :] + arrived[at, :].astype(jnp.float32)
    out[...] = (total + crossed[...].astype(jnp.float32)).astype(jnp.bfloat16)


def combine_kernel(rounds, weighted, residual, *refs):
    backs, (mine, send, total) = refs[:rounds], refs[rounds:]
    feat = residual.shape[1]
    core = position()[1]
    rows = jnp.concatenate([b[...].astype(jnp.float32) for b in backs], axis=0)
    total[...] = lax.dot_general(
        weighted[...],
        rows,
        (((0,), (0,)), ((), ())),
        precision=lax.Precision.HIGHEST,
        preferred_element_type=jnp.float32,
    )
    here = pl.ds(pl.multiple_of(core * feat, 128), feat)
    away = pl.ds(pl.multiple_of((1 - core) * feat, 128), feat)
    mine[...] = residual[...].astype(jnp.float32) + total[:, here]
    send[...] = total[:, away]


def held(*shape, dtype=jnp.bfloat16):
    return pltpu.VMEM(shape, dtype)


def in_vmem(v):
    return pltpu.with_memory_space_constraint(v, pltpu.VMEM)


def in_hbm(v):
    return pltpu.with_memory_space_constraint(v, pltpu.HBM)


def call(body, args, specs, outs, scratch=(), mib=2, flops=0, moved=0, alias=None):
    return pl.pallas_call(
        body,
        out_shape=outs,
        in_specs=specs,
        out_specs=[IN_VMEM] * len(outs),
        scratch_shapes=list(scratch),
        compiler_params=pltpu.CompilerParams(vmem_limit_bytes=mib << 20),
        cost_estimate=pl.CostEstimate(
            flops=int(flops), bytes_accessed=int(moved), transcendentals=0
        ),
        input_output_aliases=alias or {},
    )(*args)


def expert_layer(
    moe_input, norm_gain, expert_ids, combine_weights, capacity, w_gate, w_up, w_down
):
    devices, members = lax.axis_size("expert"), lax.axis_size("mp")
    tokens, feat = moe_input.shape
    split = devices // capacity.shape[0]
    slots = tokens // 2
    rounds = devices // 2
    rows = rounds * slots
    width, depth = 2 * feat, members * feat
    hid = w_gate.shape[2]
    order = range(rounds)
    f32 = jnp.float32

    def across(v, bit):
        return lax.ppermute(v, "mp", [(i, i ^ bit) for i in range(members)])

    def between(v, k):
        pairs = [
            (e * members + m, (e ^ (2 * k + m % 2)) * members + m)
            for e in range(devices)
            for m in range(members)
        ]
        return lax.ppermute(v, ("expert", "mp"), pairs)

    low = rounds // 2
    sibling = across(moe_input, 1)
    opposite = across(moe_input, 2)
    select, weighted = call(
        functools.partial(route_kernel, slots, split),
        [in_hbm(expert_ids.T), in_hbm(combine_weights.T), in_hbm(capacity)],
        [IN_PLACE] * 3,
        [held(rows, tokens), held(rows, tokens, dtype=f32)],
        scratch=[
            pltpu.VMEM((TOP, tokens), jnp.int32),
            pltpu.VMEM((TOP, tokens), f32),
            pltpu.SMEM(capacity.shape, jnp.int32),
            pltpu.SemaphoreType.DMA((3,)),
        ],
        flops=ROUTE_FLOPS,
        moved=1e5,
    )
    gain, select = lax.optimization_barrier((norm_gain, select))
    gain = gain[None, :]
    gain, sibling, select = lax.optimization_barrier((gain, sibling, select))

    def pack(first, count, total, sources):
        return call(
            functools.partial(pack_kernel, slots, first, total),
            [select, *sources],
            [IN_VMEM] * (1 + len(sources)),
            [held(slots, total)] * count,
            flops=PACK_FLOPS,
            moved=1e6,
        )

    high_sends = pack(low, rounds - low, width, [moe_input, sibling])
    near = [between(high_sends[k - low], k) for k in range(low, rounds)]
    diagonal = across(opposite, 1)
    low_sends = pack(0, low, depth, [moe_input, sibling, opposite, diagonal])
    full = [between(low_sends[k], k) for k in range(low)]

    gain, _ = lax.optimization_barrier((gain, high_sends[0]))
    gain_sib = across(gain, 1)
    gain_far = across(gain, 2)
    gain_both = across(gain_far, 1)
    (gains,) = call(
        gain_kernel,
        [gain, gain_sib, gain_far, gain_both],
        [IN_VMEM] * 4,
        [held(1, depth, dtype=f32)],
    )

    def norm(parts):
        return call(
            norm_kernel,
            [*parts, gains],
            [IN_VMEM] * (len(parts) + 1),
            [held(slots, depth)],
            flops=8 * slots * depth,
            moved=4 * slots * depth,
        )[0]

    normed = [norm([part]) for part in full]
    far = [across(part, 2) for part in near]
    far[:-1], normed = lax.optimization_barrier((far[:-1], normed))
    normed += [norm([here, there]) for here, there in zip(near, far)]
    traded = [across(v, 1) for v in normed]
    entering = [in_vmem(v) for v in normed + traded]
    blocks = hid // DEEP
    early, later = min(EARLY, blocks - 1), min(LATER, blocks - 1)
    weight = in_hbm(w_down[0])
    hidden, ahead = call(
        functools.partial(hidden_kernel, len(entering)),
        [*entering, in_vmem(w_gate[0]), in_vmem(w_up[0]), weight],
        [IN_VMEM] * (len(entering) + 2) + [IN_PLACE],
        [held(2 * rows, hid), held(early * DEEP, width)],
        scratch=[pltpu.SemaphoreType.DMA((early,))],
        flops=8 * rows * depth * hid,
        moved=2 * early * DEEP * width,
    )

    def down(first, ready, later):
        missing = blocks - ready.shape[0] // DEEP
        ahead = [held(later * DEEP, width)] if later else []
        sems = [pltpu.SemaphoreType.DMA((later,))] if later else []
        return call(
            functools.partial(down_kernel, first, later),
            [in_vmem(hidden), in_vmem(ready), weight],
            [IN_VMEM] * 2 + [IN_PLACE],
            [held(rows, width, dtype=f32), held(rows, width)] + ahead,
            scratch=[
                pltpu.VMEM((missing * DEEP, width), jnp.bfloat16),
                pltpu.VMEM((2 * rows, width), f32),
                pltpu.SemaphoreType.DMA((missing,)),
            ]
            + sems,
            mib=3 + missing * DEEP * width * 2 // 2**20 + 1,
            flops=2 * rows * depth * hid,
            moved=2 * (missing + later) * DEEP * width,
        )

    own_far, sib_far, kept = down(0, ahead, later)
    arrived_far = across(sib_far, 1)
    own_near, sib_near = down(blocks, kept, 0)
    arrived_near = across(sib_near, 1)
    crossing = call(
        merge_kernel,
        [own_far, arrived_far],
        [IN_VMEM] * 2,
        [held(slots, width)] * rounds,
        flops=rows * width,
        moved=8 * rows * width,
    )
    backs = []
    for k in reversed(order):
        (summed,) = call(
            functools.partial(fold_kernel, k),
            [own_near, arrived_near, across(crossing[k], 2)],
            [IN_VMEM] * 3,
            [held(slots, width)],
            flops=slots * width,
            moved=8 * slots * width,
        )
        backs.insert(0, between(summed, k))
    mine, send = call(
        functools.partial(combine_kernel, rounds),
        [weighted, moe_input, *backs],
        [IN_VMEM] * (2 + rounds),
        [held(tokens, feat, dtype=f32)] * 2,
        scratch=[pltpu.VMEM((tokens, width), f32)],
        mib=4,
        flops=2 * rows * tokens * width,
        moved=4 * rows * width,
    )
    return (mine + across(send, 1)).astype(jnp.bfloat16)


def gathered_layer(
    moe_input, norm_gain, expert_ids, combine_weights, capacity, w_gate, w_up, w_down
):
    tok_rows, feat_width = moe_input.shape
    experts = capacity.shape[0]
    depth = feat_width * lax.axis_size("mp")
    experts_total = lax.axis_size("expert")
    split_count = experts_total // experts
    slot_count = tok_rows // 2
    residual = moe_input.astype(jnp.float32)
    square_sum = lax.psum(jnp.sum(residual * residual, axis=1), "mp")
    normed = (
        residual * lax.rsqrt(square_sum / depth + 1e-05)[:, None] * norm_gain[None, :]
    ).astype(jnp.bfloat16)
    flat_ids = expert_ids.reshape(-1)
    one_hot = (flat_ids[:, None] == jnp.arange(experts)[None, :]).astype(jnp.int32)
    earlier = jnp.cumsum(one_hot, axis=0) - one_hot
    slot_rank = jnp.sum(earlier * one_hot, axis=1)
    limits = jnp.sum(one_hot * capacity[None, :], axis=1)
    kept_mask = slot_rank < limits
    slot_id = flat_ids * slot_count + slot_rank
    select = (jnp.arange(experts * slot_count)[:, None] == slot_id[None, :]) & kept_mask[None, :]
    chosen = select.reshape(experts * slot_count, tok_rows, TOP).sum(axis=-1).astype(jnp.bfloat16)
    packed = jnp.dot(chosen, normed, preferred_element_type=jnp.float32).astype(jnp.bfloat16)
    packed_view = packed.reshape(experts, 1, slot_count, feat_width)
    outgoing = jnp.broadcast_to(
        packed_view, (experts, split_count, slot_count, feat_width)
    ).reshape(experts_total, slot_count, feat_width)
    arrived = lax.all_to_all(outgoing, "expert", split_axis=0, concat_axis=0, tiled=True)
    slot_rows = arrived.reshape(experts_total * slot_count, feat_width)
    piece = lax.all_gather(slot_rows, "mp", axis=1, tiled=True)
    gate_sum = jnp.dot(piece, w_gate[0], preferred_element_type=jnp.float32)
    up_sum = jnp.dot(piece, w_up[0], preferred_element_type=jnp.float32)
    hidden = (jax.nn.silu(gate_sum) * up_sum).astype(jnp.bfloat16)
    down_terms = jnp.dot(hidden, w_down[0], preferred_element_type=jnp.float32)
    result = lax.psum_scatter(
        down_terms.astype(jnp.bfloat16), "mp", scatter_dimension=1, tiled=True
    )
    result = result.reshape(experts_total, slot_count, feat_width)
    returned = lax.all_to_all(result, "expert", split_axis=0, concat_axis=0, tiled=True)
    gathered = (
        returned.astype(jnp.float32)
        .reshape(experts, split_count, slot_count, feat_width)
        .sum(axis=1)
    )
    weighted = select.astype(jnp.float32) * combine_weights.reshape(-1)[None, :]
    weighted = weighted.reshape(experts * slot_count, tok_rows, TOP).sum(axis=-1)
    added = jnp.dot(
        weighted.T,
        gathered.reshape(experts * slot_count, feat_width),
        precision=lax.Precision.HIGHEST,
        preferred_element_type=jnp.float32,
    )
    return (residual + added).astype(jnp.bfloat16)


def attend_held(queries, k_cache, v_cache, lengths):
    seqs, heads, size = queries.shape
    tall = -(-heads // 16) * 16
    flat = queries.transpose(1, 0, 2).reshape(heads * seqs, size)
    positions = k_cache.shape[2]
    (out,) = call(
        functools.partial(attend_kernel, size ** (-0.5), seqs),
        [in_hbm(v) for v in (lengths, flat, k_cache, v_cache)],
        [IN_PLACE] * 4,
        [held(heads * seqs, size)],
        scratch=[
            pltpu.SMEM(lengths.shape, jnp.int32),
            pltpu.VMEM(flat.shape, flat.dtype),
            pltpu.VMEM((RING, SPAN) + k_cache.shape[1:], k_cache.dtype),
            pltpu.VMEM((tall * seqs, size), jnp.float32),
            pltpu.VMEM((tall * seqs, positions), jnp.float32),
            pltpu.VMEM((tall * seqs, positions), jnp.bfloat16),
            pltpu.SemaphoreType.DMA((2 + 2 * (seqs // SPAN),)),
        ],
        mib=7,
        flops=8 * seqs * tall * size * positions,
        moved=2 * k_cache.size * 2,
    )
    return out.reshape(heads, seqs, size).transpose(1, 0, 2)


def on_device(queries, k_cache, v_cache, lengths, moe_input, *rest):
    arriving = lax.axis_size("expert") * (moe_input.shape[0] // 2)
    paired = lax.axis_size("mp") == 4 and lax.axis_size("expert") % 4 == 0
    if paired and arriving <= VMEM_ROWS:
        context = attend_held(queries, k_cache, v_cache, lengths)
        return context, expert_layer(moe_input, *rest)
    context = attention(queries, k_cache, v_cache, lengths)
    return context, gathered_layer(moe_input, *rest)


def solution(mesh):
    in_specs = (
        P("expert", "mp", None),
        P("expert", "mp", None, None),
        P("expert", "mp", None, None),
        P("expert"),
        P("expert", "mp"),
        P("mp"),
        P("expert", None),
        P("expert", None),
        P(),
        P("expert", None, "mp"),
        P("expert", None, "mp"),
        P("expert", "mp", None),
    )
    out_specs = (P("expert", "mp", None), P("expert", "mp"))
    return jax.shard_map(
        on_device, mesh=mesh, in_specs=in_specs, out_specs=out_specs, check_vma=False
    )
```

```python
import functools

import jax
import jax.numpy as jnp
from jax import lax
from jax.experimental import pallas as pl
from jax.experimental.pallas import tpu as pltpu
from jax.sharding import PartitionSpec as P


TOP = 2
WIDE = 512
DEEP = 256
EARLY = 7
LATER = 3
VMEM_ROWS = 128
ROUTE_FLOPS = 2e10
PACK_FLOPS = 2e10


IN_VMEM = pl.BlockSpec(memory_space=pltpu.VMEM)
IN_PLACE = pl.BlockSpec(memory_space=pl.ANY)


def attention(queries, k_cache, v_cache, lengths):
    seq_count, head_count, head_size = queries.shape
    kv_count = k_cache.shape[1]
    group_size = head_count // kv_count
    queries_grouped = queries.reshape(seq_count, kv_count, group_size, head_size)
    scores = jnp.einsum(
        "bjgd,bjpd->bjgp", queries_grouped, k_cache, preferred_element_type=jnp.float32
    ) * head_size ** (-0.5)
    positions = jnp.arange(k_cache.shape[2])
    live_mask = positions[None, :] < lengths[:, None]
    scores = jnp.where(live_mask[:, None, None, :], scores, -jnp.inf)
    top_score = jnp.max(scores, axis=-1, keepdims=True)
    expo = jnp.exp(scores - top_score)
    probs = (expo / jnp.sum(expo, axis=-1, keepdims=True)).astype(jnp.bfloat16)
    context = jnp.einsum("bjgp,bjpd->bjgd", probs, v_cache, preferred_element_type=jnp.float32)
    return context.astype(jnp.bfloat16).reshape(seq_count, head_count, head_size)


def attend_kernel(scale, seqs, lengths_at, q_at, k, v, out, lengths, q, wide, score, prob, sems):
    near = [
        pltpu.make_async_copy(source, target, sems.at[i])
        for i, (source, target) in enumerate(((lengths_at, lengths), (q_at, q)))
    ]
    for copy in near:
        copy.start()
    heads, size = q.shape[0] // seqs, q.shape[1]
    kv, positions = k.shape[1], k.shape[2]
    tall = wide.shape[0] // seqs
    group = heads // kv
    row = lax.broadcasted_iota(jnp.int32, (tall, positions), 0)
    lane = lax.broadcasted_iota(jnp.int32, (tall, positions), 1)
    for copy in near:
        copy.wait()
    wide[: heads * seqs, :] = q[...].astype(jnp.float32)
    wide[heads * seqs :, :] = jnp.zeros(((tall - heads) * seqs, size), jnp.float32)
    for b in range(seqs):
        queries = wide[pl.ds(b, tall, stride=seqs), :].astype(jnp.bfloat16)
        total = None
        for j in range(kv):
            dots = lax.dot_general(
                queries, k[b, j], (((1,), (1,)), ((), ())), preferred_element_type=jnp.float32
            )
            total = dots if total is None else jnp.where(row < j * group, total, dots)
        live = lane < lengths[b]
        score[b * tall : (b + 1) * tall, :] = jnp.where(live, total * scale, -jnp.inf)
    top = jnp.max(score[...], axis=-1, keepdims=True)
    expo = jnp.exp(score[...] - top)
    prob[...] = (expo / jnp.sum(expo, axis=-1, keepdims=True)).astype(jnp.bfloat16)
    for b in range(seqs):
        probs = prob[b * tall : (b + 1) * tall, :].astype(jnp.float32)
        total = jnp.zeros((tall, size), jnp.float32)
        for j in range(kv):
            mine = (row >= j * group) & (row < (j + 1) * group)
            total = total + jnp.dot(
                jnp.where(mine, probs, 0.0).astype(jnp.bfloat16),
                v[b, j],
                preferred_element_type=jnp.float32,
            )
        wide[pl.ds(b, tall, stride=seqs), :] = total
    out[...] = wide[: heads * seqs, :].astype(jnp.bfloat16)


def position():
    member = lax.axis_index("mp")
    return member, member % 2, member // 2


def route_kernel(slots, split, ids_at, weights_at, cap_at, select, weighted, ids, weights, cap, sems):
    loads = [
        pltpu.make_async_copy(ids_at, ids, sems.at[0]),
        pltpu.make_async_copy(weights_at, weights, sems.at[1]),
        pltpu.make_async_copy(cap_at, cap, sems.at[2]),
    ]
    for load in loads:
        load.start()
    core, block = position()[1], lax.axis_index("expert")
    rows, tokens = select.shape
    row = lax.broadcasted_iota(jnp.int32, (rows, tokens), 0)
    step = row // slots
    slot = row - step * slots
    expert = jnp.bitwise_xor(block, 2 * step + core) // split
    before = lax.broadcasted_iota(jnp.int32, (tokens, tokens), 0)
    after = lax.broadcasted_iota(jnp.int32, (tokens, tokens), 1)
    earlier = (before < after).astype(jnp.float32)
    for load in loads:
        load.wait()
    first = ids[0:1, :] == expert
    named = first | (ids[1:2, :] == expert)
    rank = jnp.dot(named.astype(jnp.float32), earlier, preferred_element_type=jnp.float32)
    rank = rank.astype(jnp.int32)
    limit = jnp.zeros((rows, tokens), jnp.int32)
    for e in range(cap.shape[0]):
        limit = jnp.where(expert == e, cap[e], limit)
    chosen = named & (rank == slot) & (rank < limit)
    weighted[...] = jnp.where(
        chosen, jnp.where(first, weights[0:1, :], weights[1:2, :]), 0.0
    )
    select[...] = chosen.astype(jnp.float32).astype(jnp.bfloat16)


def pack_kernel(slots, first, width, select, *refs):
    sources, sends = refs[: width // refs[0].shape[1]], refs[width // refs[0].shape[1] :]
    member = position()[0]
    feat = sources[0].shape[1]
    rows = select[first * slots : (first + len(sends)) * slots, :]
    for i, source in enumerate(sources):
        moved = jnp.dot(rows, source[...], preferred_element_type=jnp.float32)
        moved = moved.astype(jnp.bfloat16)
        place = lax.rem(jnp.bitwise_xor(member, i) * feat, width)
        columns = pl.ds(pl.multiple_of(place, 128), feat)
        for k, send in enumerate(sends):
            send[:, columns] = moved[k * slots : (k + 1) * slots, :]


def gain_kernel(own, sibling, across, both, out):
    member = position()[0]
    feat = own.shape[1]
    for i, part in enumerate((own, sibling, across, both)):
        place = jnp.bitwise_xor(member, i)
        out[:, pl.ds(pl.multiple_of(place * feat, 128), feat)] = part[...]


def norm_kernel(*refs):
    parts, (gain, out) = refs[:-2], refs[-2:]
    plane = position()[2]
    width, depth = parts[0].shape[1], out.shape[1]
    starts = (plane * width, (1 - plane) * width) if len(parts) == 2 else (0,)
    total = jnp.zeros((out.shape[0], 128), jnp.float32)
    for part in parts:
        for j in range(width // 128):
            v = part[:, j * 128 : (j + 1) * 128].astype(jnp.float32)
            total = total + v * v
    mean = jnp.sum(total, axis=1, keepdims=True) / depth
    scale = lax.rsqrt(mean + 1e-05)
    for part, start in zip(parts, starts):
        for j in range(0, width, WIDE):
            columns = pl.ds(pl.multiple_of(start + j, 128), WIDE)
            v = part[:, j : j + WIDE].astype(jnp.float32)
            out[:, columns] = (v * scale * gain[:, columns]).astype(jnp.bfloat16)


def half_load(w_down, target, sems, first):
    width = w_down.shape[1] // 2
    blocks = w_down.shape[0] // DEEP
    plane = position()[2]

    def load(i):
        half, block = divmod(first + i, blocks)
        start = (plane if half else 1 - plane) * width
        return pltpu.make_async_copy(
            w_down.at[block * DEEP : (block + 1) * DEEP, pl.ds(pl.multiple_of(start, 128), width)],
            target.at[i * DEEP : (i + 1) * DEEP, :],
            sems.at[i],
        )

    return load


def hidden_kernel(count, *refs):
    rows_in, (w_gate, w_up, w_down, hidden, ahead, sems) = refs[:count], refs[count:]
    load = half_load(w_down, ahead, sems, 0)
    blocks = sems.shape[0]
    for i in range(blocks):
        load(i).start()

    @pl.loop(0, w_gate.shape[1] // WIDE)
    def _(j):
        columns = pl.ds(pl.multiple_of(j * WIDE, WIDE), WIDE)
        rows = jnp.concatenate([r[...] for r in rows_in], axis=0)
        gate = jnp.dot(rows, w_gate[:, columns], preferred_element_type=jnp.float32)
        up = jnp.dot(rows, w_up[:, columns], preferred_element_type=jnp.float32)
        hidden[:, columns] = (gate / (1.0 + jnp.exp(-gate)) * up).astype(jnp.bfloat16)

    for i in range(blocks):
        load(i).wait()


def down_kernel(first, later, hidden, ready, w_down, own, sib, *refs):
    if later:
        ahead, here, total, sems, sems_later = refs
    else:
        here, total, sems = refs
    half, width = own.shape
    known, missing = ready.shape[0], sems.shape[0]
    load = half_load(w_down, here, sems, first + known // DEEP)
    for i in range(missing):
        load(i).start()
    if later:
        load_later = half_load(w_down, ahead, sems_later, first + known // DEEP + missing)
        for i in range(later):
            load_later(i).start()
    for step in range(missing + 1):
        if step == 0:
            left, weight = hidden.at[:, :known], ready
        else:
            load(step - 1).wait()
            at = known + (step - 1) * DEEP
            left = hidden.at[:, at : at + DEEP]
            weight = here.at[(step - 1) * DEEP : step * DEEP, :]
        for j in range(width // WIDE):
            columns = slice(j * WIDE, (j + 1) * WIDE)
            out = jnp.dot(left[...], weight[:, columns], preferred_element_type=jnp.float32)
            if step > 0:
                out = out + total[:, columns]
            if step < missing:
                total[:, columns] = out
            else:
                own[:, columns] = out[:half, :]
                sib[:, columns] = out[half:, :].astype(jnp.bfloat16)
    if later:
        for i in range(later):
            load_later(i).wait()


def merge_kernel(own, arrived, *sends):
    slots = sends[0].shape[0]
    for k, send in enumerate(sends):
        at = slice(k * slots, (k + 1) * slots)
        send[...] = (own[at, :] + arrived[at, :].astype(jnp.float32)).astype(jnp.bfloat16)


def fold_kernel(k, own, arrived, crossed, out):
    slots = out.shape[0]
    at = slice(k * slots, (k + 1) * slots)
    total = own[at, :] + arrived[at, :].astype(jnp.float32)
    out[...] = (total + crossed[...].astype(jnp.float32)).astype(jnp.bfloat16)


def combine_kernel(rounds, weighted, residual, *refs):
    backs, (mine, send, total) = refs[:rounds], refs[rounds:]
    feat = residual.shape[1]
    core = position()[1]
    rows = jnp.concatenate([b[...].astype(jnp.float32) for b in backs], axis=0)
    total[...] = lax.dot_general(
        weighted[...],
        rows,
        (((0,), (0,)), ((), ())),
        precision=lax.Precision.HIGHEST,
        preferred_element_type=jnp.float32,
    )
    here = pl.ds(pl.multiple_of(core * feat, 128), feat)
    away = pl.ds(pl.multiple_of((1 - core) * feat, 128), feat)
    mine[...] = residual[...].astype(jnp.float32) + total[:, here]
    send[...] = total[:, away]


def held(*shape, dtype=jnp.bfloat16):
    return pltpu.VMEM(shape, dtype)


def in_vmem(v):
    return pltpu.with_memory_space_constraint(v, pltpu.VMEM)


def in_hbm(v):
    return pltpu.with_memory_space_constraint(v, pltpu.HBM)


def call(body, args, specs, outs, scratch=(), mib=2, flops=0, moved=0, alias=None):
    return pl.pallas_call(
        body,
        out_shape=outs,
        in_specs=specs,
        out_specs=[IN_VMEM] * len(outs),
        scratch_shapes=list(scratch),
        compiler_params=pltpu.CompilerParams(vmem_limit_bytes=mib << 20),
        cost_estimate=pl.CostEstimate(
            flops=int(flops), bytes_accessed=int(moved), transcendentals=0
        ),
        input_output_aliases=alias or {},
    )(*args)


def expert_layer(
    moe_input, norm_gain, expert_ids, combine_weights, capacity, w_gate, w_up, w_down
):
    devices, members = lax.axis_size("expert"), lax.axis_size("mp")
    tokens, feat = moe_input.shape
    split = devices // capacity.shape[0]
    slots = tokens // 2
    rounds = devices // 2
    rows = rounds * slots
    width, depth = 2 * feat, members * feat
    hid = w_gate.shape[2]
    order = range(rounds)
    f32 = jnp.float32

    def across(v, bit):
        return lax.ppermute(v, "mp", [(i, i ^ bit) for i in range(members)])

    def between(v, k):
        pairs = [
            (e * members + m, (e ^ (2 * k + m % 2)) * members + m)
            for e in range(devices)
            for m in range(members)
        ]
        return lax.ppermute(v, ("expert", "mp"), pairs)

    low = rounds // 2
    sibling = across(moe_input, 1)
    opposite = across(moe_input, 2)
    select, weighted = call(
        functools.partial(route_kernel, slots, split),
        [in_hbm(expert_ids.T), in_hbm(combine_weights.T), in_hbm(capacity)],
        [IN_PLACE] * 3,
        [held(rows, tokens), held(rows, tokens, dtype=f32)],
        scratch=[
            pltpu.VMEM((TOP, tokens), jnp.int32),
            pltpu.VMEM((TOP, tokens), f32),
            pltpu.SMEM(capacity.shape, jnp.int32),
            pltpu.SemaphoreType.DMA((3,)),
        ],
        flops=ROUTE_FLOPS,
        moved=1e5,
    )
    gain, select = lax.optimization_barrier((norm_gain, select))
    gain = gain[None, :]
    gain, sibling, select = lax.optimization_barrier((gain, sibling, select))

    def pack(first, count, total, sources):
        return call(
            functools.partial(pack_kernel, slots, first, total),
            [select, *sources],
            [IN_VMEM] * (1 + len(sources)),
            [held(slots, total)] * count,
            flops=PACK_FLOPS,
            moved=1e6,
        )

    high_sends = pack(low, rounds - low, width, [moe_input, sibling])
    near = [between(high_sends[k - low], k) for k in range(low, rounds)]
    diagonal = across(opposite, 1)
    low_sends = pack(0, low, depth, [moe_input, sibling, opposite, diagonal])
    full = [between(low_sends[k], k) for k in range(low)]

    gain, _ = lax.optimization_barrier((gain, high_sends[0]))
    gain_sib = across(gain, 1)
    gain_far = across(gain, 2)
    gain_both = across(gain_far, 1)
    (gains,) = call(
        gain_kernel,
        [gain, gain_sib, gain_far, gain_both],
        [IN_VMEM] * 4,
        [held(1, depth, dtype=f32)],
    )

    def norm(parts):
        return call(
            norm_kernel,
            [*parts, gains],
            [IN_VMEM] * (len(parts) + 1),
            [held(slots, depth)],
            flops=8 * slots * depth,
            moved=4 * slots * depth,
        )[0]

    normed = [norm([part]) for part in full]
    far = [across(part, 2) for part in near]
    far[:-1], normed = lax.optimization_barrier((far[:-1], normed))
    normed += [norm([here, there]) for here, there in zip(near, far)]
    traded = [across(v, 1) for v in normed]
    entering = [in_vmem(v) for v in normed + traded]
    blocks = hid // DEEP
    early, later = min(EARLY, blocks - 1), min(LATER, blocks - 1)
    weight = in_hbm(w_down[0])
    hidden, ahead = call(
        functools.partial(hidden_kernel, len(entering)),
        [*entering, in_vmem(w_gate[0]), in_vmem(w_up[0]), weight],
        [IN_VMEM] * (len(entering) + 2) + [IN_PLACE],
        [held(2 * rows, hid), held(early * DEEP, width)],
        scratch=[pltpu.SemaphoreType.DMA((early,))],
        flops=8 * rows * depth * hid,
        moved=2 * early * DEEP * width,
    )

    def down(first, ready, later):
        missing = blocks - ready.shape[0] // DEEP
        ahead = [held(later * DEEP, width)] if later else []
        sems = [pltpu.SemaphoreType.DMA((later,))] if later else []
        return call(
            functools.partial(down_kernel, first, later),
            [in_vmem(hidden), in_vmem(ready), weight],
            [IN_VMEM] * 2 + [IN_PLACE],
            [held(rows, width, dtype=f32), held(rows, width)] + ahead,
            scratch=[
                pltpu.VMEM((missing * DEEP, width), jnp.bfloat16),
                pltpu.VMEM((2 * rows, width), f32),
                pltpu.SemaphoreType.DMA((missing,)),
            ]
            + sems,
            mib=3 + missing * DEEP * width * 2 // 2**20 + 1,
            flops=2 * rows * depth * hid,
            moved=2 * (missing + later) * DEEP * width,
        )

    own_far, sib_far, kept = down(0, ahead, later)
    arrived_far = across(sib_far, 1)
    own_near, sib_near = down(blocks, kept, 0)
    arrived_near = across(sib_near, 1)
    crossing = call(
        merge_kernel,
        [own_far, arrived_far],
        [IN_VMEM] * 2,
        [held(slots, width)] * rounds,
        flops=rows * width,
        moved=8 * rows * width,
    )
    backs = []
    for k in reversed(order):
        (summed,) = call(
            functools.partial(fold_kernel, k),
            [own_near, arrived_near, across(crossing[k], 2)],
            [IN_VMEM] * 3,
            [held(slots, width)],
            flops=slots * width,
            moved=8 * slots * width,
        )
        backs.insert(0, between(summed, k))
    mine, send = call(
        functools.partial(combine_kernel, rounds),
        [weighted, moe_input, *backs],
        [IN_VMEM] * (2 + rounds),
        [held(tokens, feat, dtype=f32)] * 2,
        scratch=[pltpu.VMEM((tokens, width), f32)],
        mib=4,
        flops=2 * rows * tokens * width,
        moved=4 * rows * width,
    )
    return (mine + across(send, 1)).astype(jnp.bfloat16)


def gathered_layer(
    moe_input, norm_gain, expert_ids, combine_weights, capacity, w_gate, w_up, w_down
):
    tok_rows, feat_width = moe_input.shape
    experts = capacity.shape[0]
    depth = feat_width * lax.axis_size("mp")
    experts_total = lax.axis_size("expert")
    split_count = experts_total // experts
    slot_count = tok_rows // 2
    residual = moe_input.astype(jnp.float32)
    square_sum = lax.psum(jnp.sum(residual * residual, axis=1), "mp")
    normed = (
        residual * lax.rsqrt(square_sum / depth + 1e-05)[:, None] * norm_gain[None, :]
    ).astype(jnp.bfloat16)
    flat_ids = expert_ids.reshape(-1)
    one_hot = (flat_ids[:, None] == jnp.arange(experts)[None, :]).astype(jnp.int32)
    earlier = jnp.cumsum(one_hot, axis=0) - one_hot
    slot_rank = jnp.sum(earlier * one_hot, axis=1)
    limits = jnp.sum(one_hot * capacity[None, :], axis=1)
    kept_mask = slot_rank < limits
    slot_id = flat_ids * slot_count + slot_rank
    select = (jnp.arange(experts * slot_count)[:, None] == slot_id[None, :]) & kept_mask[None, :]
    chosen = select.reshape(experts * slot_count, tok_rows, TOP).sum(axis=-1).astype(jnp.bfloat16)
    packed = jnp.dot(chosen, normed, preferred_element_type=jnp.float32).astype(jnp.bfloat16)
    packed_view = packed.reshape(experts, 1, slot_count, feat_width)
    outgoing = jnp.broadcast_to(
        packed_view, (experts, split_count, slot_count, feat_width)
    ).reshape(experts_total, slot_count, feat_width)
    arrived = lax.all_to_all(outgoing, "expert", split_axis=0, concat_axis=0, tiled=True)
    slot_rows = arrived.reshape(experts_total * slot_count, feat_width)
    piece = lax.all_gather(slot_rows, "mp", axis=1, tiled=True)
    gate_sum = jnp.dot(piece, w_gate[0], preferred_element_type=jnp.float32)
    up_sum = jnp.dot(piece, w_up[0], preferred_element_type=jnp.float32)
    hidden = (jax.nn.silu(gate_sum) * up_sum).astype(jnp.bfloat16)
    down_terms = jnp.dot(hidden, w_down[0], preferred_element_type=jnp.float32)
    result = lax.psum_scatter(
        down_terms.astype(jnp.bfloat16), "mp", scatter_dimension=1, tiled=True
    )
    result = result.reshape(experts_total, slot_count, feat_width)
    returned = lax.all_to_all(result, "expert", split_axis=0, concat_axis=0, tiled=True)
    gathered = (
        returned.astype(jnp.float32)
        .reshape(experts, split_count, slot_count, feat_width)
        .sum(axis=1)
    )
    weighted = select.astype(jnp.float32) * combine_weights.reshape(-1)[None, :]
    weighted = weighted.reshape(experts * slot_count, tok_rows, TOP).sum(axis=-1)
    added = jnp.dot(
        weighted.T,
        gathered.reshape(experts * slot_count, feat_width),
        precision=lax.Precision.HIGHEST,
        preferred_element_type=jnp.float32,
    )
    return (residual + added).astype(jnp.bfloat16)


def attend_held(queries, k_cache, v_cache, lengths):
    seqs, heads, size = queries.shape
    tall = -(-heads // 16) * 16
    flat = queries.transpose(1, 0, 2).reshape(heads * seqs, size)
    positions = k_cache.shape[2]
    (out,) = call(
        functools.partial(attend_kernel, size ** (-0.5), seqs),
        [in_hbm(lengths), in_hbm(flat), in_vmem(k_cache), in_vmem(v_cache)],
        [IN_PLACE] * 2 + [IN_VMEM] * 2,
        [held(heads * seqs, size)],
        scratch=[
            pltpu.SMEM(lengths.shape, jnp.int32),
            pltpu.VMEM(flat.shape, flat.dtype),
            pltpu.VMEM((tall * seqs, size), jnp.float32),
            pltpu.VMEM((tall * seqs, positions), jnp.float32),
            pltpu.VMEM((tall * seqs, positions), jnp.bfloat16),
            pltpu.SemaphoreType.DMA((2,)),
        ],
        mib=3,
        flops=8 * seqs * tall * size * positions,
        moved=2 * k_cache.size * 2,
    )
    return out.reshape(heads, seqs, size).transpose(1, 0, 2)


def on_device(queries, k_cache, v_cache, lengths, moe_input, *rest):
    arriving = lax.axis_size("expert") * (moe_input.shape[0] // 2)
    paired = lax.axis_size("mp") == 4 and lax.axis_size("expert") % 4 == 0
    if paired and arriving <= VMEM_ROWS:
        context = attend_held(queries, k_cache, v_cache, lengths)
        return context, expert_layer(moe_input, *rest)
    context = attention(queries, k_cache, v_cache, lengths)
    return context, gathered_layer(moe_input, *rest)


def solution(mesh):
    in_specs = (
        P("expert", "mp", None),
        P("expert", "mp", None, None),
        P("expert", "mp", None, None),
        P("expert"),
        P("expert", "mp"),
        P("mp"),
        P("expert", None),
        P("expert", None),
        P(),
        P("expert", None, "mp"),
        P("expert", None, "mp"),
        P("expert", "mp", None),
    )
    out_specs = (P("expert", "mp", None), P("expert", "mp"))
    return jax.shard_map(
        on_device, mesh=mesh, in_specs=in_specs, out_specs=out_specs, check_vma=False
    )
```
